256 devices in a mesh: blk: 128 (over x_lo, z, y, core), grp: 2 (over x_hi).
Axes of the slice: x: 4 (x_hi: 2, x_lo: 2; x = x_hi * 2 + x_lo), y: 4, z: 8, core: 2. Of those that a mesh axis runs over, the one named last changes fastest.
Arguments:
- points: float32 [32768, 4096], P(('blk', 'grp')), may hold values from -40 to 40
- cand_index: int32 [256, 128], P(('blk', 'grp')), may hold values from 0 to 127, as said below
- cand_count: int32 [256], P(('blk', 'grp')), may hold values from 32 to 128
- neighbor_ids: int32 [32768, 16], P(('blk', 'grp')), may hold values from 0 to 32767
- old_dist: float32 [32768, 16], P(('blk', 'grp')), may hold values from 0.3 to 10
Outputs:
- scaled_dist: float32 [32768, 16], P(('blk', 'grp'))
The draws below stay inside these ranges and needn't reach their ends.
Inputs may be any that keep to these rules, and one draw needn't show every extreme that they name: `cand_index`: within each row, distinct indices of rows of the block.
All inputs are finite; a program needn't handle non-finite values.
Results may differ from the reference program's by a relative error of at most 0.0003.
Values sent between devices are 32-bit elements; how exact they have to be, the bound alone decides.
A program may use at most 128 MiB of HBM per device.

```python
import math
import jax
import jax.numpy as jnp
from jax import lax

D = 4096
KNN = 16
CAND = 128
REACH = 2
PTS_DEV = 128
BLOCKS = 256
NPTS = 32768
N_BLK = 128
N_GRP = 2


def draw_points(key, part):
    keys = jax.random.split(jax.random.fold_in(key, 11), 6)
    clusters = max(2, (2 * REACH + 1) * N_GRP * CAND // (3 * KNN))
    position = jnp.arange(NPTS, dtype=jnp.float32) / NPTS
    trend = jnp.exp(0.5 * math.log(3.0) * position)
    member = jax.random.randint(keys[0], (NPTS,), 0, clusters, jnp.int32)
    centre_scale = jnp.exp(jax.random.uniform(keys[1], (clusters, 1), jnp.float32, 0.0, math.log(3.0)))
    centres = jnp.clip(jax.random.normal(keys[2], (clusters, D), jnp.float32), -4.0, 4.0)
    noise = jnp.clip(jax.random.normal(keys[4], (NPTS, D), jnp.float32), -4.0, 4.0)
    jitter = jnp.exp(jax.random.uniform(keys[5], (NPTS, 1), jnp.float32, 0.0, 0.5 * math.log(10.0)))
    placed = (centres * centre_scale)[member]
    value = placed + 0.35 * jitter * noise
    return value * trend[:, None]


def first_rows(subkey):
    return jax.random.permutation(subkey, PTS_DEV)[:CAND].astype(jnp.int32)


def draw_cand_index(key, part):
    subkeys = jax.random.split(jax.random.fold_in(key, 23), BLOCKS)
    return jax.vmap(first_rows)(subkeys)


def draw_neighbor_ids(key, part):
    first, second, third = jax.random.split(jax.random.fold_in(key, 37), 3)
    row_block = jnp.arange(NPTS, dtype=jnp.int32) // PTS_DEV
    cycle_pos = row_block // N_GRP
    offset = jax.random.randint(first, (NPTS, KNN), -REACH, REACH + 1, jnp.int32)
    member = jax.random.randint(second, (NPTS, KNN), 0, N_GRP, jnp.int32)
    within = jax.random.randint(third, (NPTS, KNN), 0, PTS_DEV, jnp.int32)
    source = (cycle_pos[:, None] + offset) % N_BLK * N_GRP + member
    return (source * PTS_DEV + within).astype(jnp.int32)


def touch_ends(result, rng, low, high):
    index_at = [jax.random.randint(jax.random.fold_in(rng, axis), (), 0, length) for axis, length in enumerate(result.shape)]
    widest = result.shape.index(max(result.shape))
    neighbour = index_at[:widest] + [(index_at[widest] + 1) % result.shape[widest]] + index_at[widest + 1:]
    return result.at[tuple(index_at)].set(low).at[tuple(neighbour)].set(high)


def level_of(stream_key, shape, cuts, low, top_value):
    def one(axis_at, blocks):
        draws = jax.random.uniform(jax.random.fold_in(jax.random.fold_in(stream_key, 6), axis_at), (blocks,), jnp.float32, low / len(cuts), top_value / len(cuts))
        return jnp.repeat(jnp.exp(draws), shape[axis_at] // blocks).reshape((-1,) + (1,) * (len(shape) - axis_at - 1))

    level = one(*cuts[0])
    for cut in cuts[1:]:
        level = level * one(*cut)
    return level


def setup_inputs(seed: int = 0) -> dict:
    splits = jax.random.split(jax.random.key(seed), 6)
    points = draw_points(jax.random.fold_in(splits[5], 71), 0)
    cand_index = draw_cand_index(jax.random.fold_in(splits[5], 71), 0)
    cand_count = touch_ends(jax.random.randint(splits[2], (BLOCKS,), CAND // 4, CAND + 1), jax.random.fold_in(splits[2], 1), CAND // 4, CAND).astype(jnp.int32)
    neighbor_ids = draw_neighbor_ids(jax.random.fold_in(splits[5], 71), 0)
    old_dist = jnp.clip(jnp.exp(math.log(10.0) - 3.506558 * jax.random.uniform(splits[4], (NPTS, KNN), jnp.float32) ** level_of(splits[4], (NPTS, KNN), ((0, 256),), -0.2, 0.2)), 0.3, 10.0)
    return dict(points=points, cand_index=cand_index, cand_count=cand_count, neighbor_ids=neighbor_ids, old_dist=old_dist)


far_value = 1e30


def pick_rows(block_points, block_index):
    return block_points[block_index]


def reference(points, cand_index, cand_count, neighbor_ids, old_dist):
    blocks = N_BLK * N_GRP
    grouped = points.reshape(blocks, PTS_DEV, D)
    slots = jnp.arange(CAND, dtype=jnp.int32)
    anchor = jnp.arange(blocks, dtype=jnp.int32)
    cand_ids = jnp.where(slots[None, :] < cand_count[:, None], anchor[:, None] * PTS_DEV + cand_index, -1).astype(jnp.int32)
    cand_rows = jax.vmap(pick_rows)(grouped, cand_index)
    cand_norms = jnp.sum(cand_rows * cand_rows, axis=2)
    offsets = jnp.arange(-REACH, REACH + 1, dtype=jnp.int32)
    members = jnp.arange(N_GRP, dtype=jnp.int32)
    lists = neighbor_ids.reshape(blocks, PTS_DEV, KNN)
    stored = old_dist.reshape(blocks, PTS_DEV, KNN)

    def one_block(block):
        cycle_pos = block // N_GRP
        sources = (((cycle_pos + offsets) % N_BLK)[:, None] * N_GRP + members[None, :]).reshape(-1)
        rows = cand_rows[sources].reshape(-1, D)
        row_ids = cand_ids[sources].reshape(-1)
        row_norms = cand_norms[sources].reshape(-1)
        local = grouped[block]
        local_norms = jnp.sum(local * local, axis=1)
        inner = jnp.dot(local, rows.T, precision=lax.Precision.HIGHEST, preferred_element_type=jnp.float32)
        distance = (local_norms[:, None] + row_norms[None, :] - 2.0 * inner) / D
        own_ids = block * PTS_DEV + jnp.arange(PTS_DEV, dtype=jnp.int32)
        known = jnp.any(lists[block][:, :, None] == row_ids[None, None, :], axis=1)
        masked = (row_ids[None, :] < 0) | (row_ids[None, :] == own_ids[:, None]) | known
        distance = jnp.where(masked, jnp.float32(far_value), distance)
        joined = jnp.concatenate([stored[block], distance], axis=1)
        return jnp.sort(joined, axis=1)[:, :KNN]

    best = lax.map(one_block, jnp.arange(blocks, dtype=jnp.int32)).reshape(NPTS, KNN)
    mean_last = jnp.sum(best[:, KNN - 1]) / NPTS
    return best / mean_last
```

```python
import functools

import jax
import jax.numpy as jnp
from jax import lax
from jax.experimental import pallas as pl
from jax.experimental.pallas import tpu as pltpu
from jax.sharding import Mesh
from jax.sharding import PartitionSpec as P

AXES = ("xl", "z", "y", "core", "grp")
SIZES = (2, 8, 4, 2, 2)
NODES = 64
MESH = pl.DeviceIdType.MESH
HIGHEST = lax.Precision.HIGHEST
PTS = 128
D = 4096
KNN = 16
QUARTER = 1024
CHUNKS = 4
WIDTH = QUARTER // CHUNKS
FAR = 1e30
DEAD = 1e35
SUM_PHASES = ((3, 0, 4), (2,), (1,))


def sort_pairs(n):
    pairs = []
    p = 1
    while p < n:
        k = p
        while k >= 1:
            for j in range(k % p, n - k, 2 * k):
                for i in range(min(k, n - j - k)):
                    if (i + j) // (2 * p) == (i + j + k) // (2 * p):
                        pairs.append((i + j, i + j + k))
            k //= 2
        p *= 2
    return pairs


SORT16 = sort_pairs(KNN)


def sort_lists(values):
    values = list(values)
    for i, j in SORT16:
        low, high = jnp.minimum(values[i], values[j]), jnp.maximum(values[i], values[j])
        values[i], values[j] = low, high
    return values


def merge_lists(a, b):
    m = [jnp.minimum(a[i], b[KNN - 1 - i]) for i in range(KNN)]
    step = KNN // 2
    while step:
        for i in range(KNN):
            if not i & step:
                low, high = jnp.minimum(m[i], m[i + step]), jnp.maximum(m[i], m[i + step])
                m[i], m[i + step] = low, high
        step //= 2
    return m


def dot_nt(a, b):
    return lax.dot_general(
        a, b, (((1,), (1,)), ((), ())), precision=HIGHEST, preferred_element_type=jnp.float32
    )


def to_lanes(block):
    wide = jnp.concatenate([block, jnp.zeros((PTS, PTS - KNN), block.dtype)], axis=1)
    return wide.T[:KNN]


def device_of(node, core, grp):
    return (node // 32, (node // 4) % 8, node % 4, core, grp)


def kernel(
    pts, cidx, ccnt, nbr, old, out,
    both, xr, fb, gx, gf, gb, gx_r, gf_r, gb_r, hx, hf, hb, rx, rv, rbv, ru,
    info, bias, tiles, nb_v, old_v, ci_v, nb_t, sum_src, sum_in,
    loc_sem, cc_v, sib_s, sib_r, x_s, x_r, yo_s, yr_s, f_r, info_s, info_r, red_s, red_r,
    t_s, rx_sem, rv_sem, rbv_sem, ru_sem, sum_s, sum_r,
):
    d = tuple(lax.axis_index(a) for a in AXES)
    c, g = d[3], d[4]
    q = d[0] * 32 + d[1] * 4 + d[2]
    up, down = (q + 1) % NODES, (q + NODES - 1) % NODES
    ahead = (q + NODES + 2 * c - 1) % NODES
    behind = (q + NODES + 1 - 2 * c) % NODES
    sibling = device_of(q, 1 - c, g)

    def remote(src, dst, send, recv, to):
        return pltpu.make_async_remote_copy(
            src_ref=src, dst_ref=dst, send_sem=send, recv_sem=recv, device_id=to, device_id_type=MESH
        )

    barrier = pltpu.get_barrier_semaphore()
    peers = [device_of(n, k, h) for n in (up, down) for k in (0, 1) for h in (0, 1)]
    sum_peers = []
    for axes in SUM_PHASES:
        count = 1
        for a in axes:
            count *= SIZES[a]
        row = []
        for offset in range(1, count):
            at, rest = list(d), offset
            for a in axes:
                at[a] = (d[a] + rest % SIZES[a]) % SIZES[a]
                rest //= SIZES[a]
            row.append(tuple(at))
        sum_peers.append(row)
        peers += row
    for peer in peers:
        pl.semaphore_signal(barrier, inc=1, device_id=peer, device_id_type=MESH)
    loads = [
        pltpu.make_async_copy(pts, both.at[c], loc_sem.at[0]),
        pltpu.make_async_copy(cidx, ci_v, loc_sem.at[1]),
        pltpu.make_async_copy(nbr, nb_v, loc_sem.at[2]),
        pltpu.make_async_copy(old, old_v, loc_sem.at[3]),
        pltpu.make_async_copy(ccnt, cc_v, loc_sem.at[4]),
    ]
    for load in loads:
        load.start()
    pl.semaphore_wait(barrier, len(peers))

    def cols(quarter, j):
        return pl.ds(pl.multiple_of(quarter * QUARTER + j * WIDTH, 128), WIDTH)

    def part(j):
        return pl.ds(j * WIDTH, WIDTH)

    def x_copy(k, j):
        return remote(
            pts.at[:, cols(2 * (1 - g) + k, j)], xr.at[c, :, part(j)], x_s.at[k, j], x_r.at[c, j],
            device_of(q, k, 1 - g),
        )

    def yo_copy(k, j):
        return remote(
            pts.at[:, cols(2 * g + k, j)], fb.at[c, g, :, part(j)], yo_s.at[k, j], f_r.at[c, g, j],
            device_of(ahead, k, g),
        )

    def sib_copy(i):
        quarter = pl.ds(pl.multiple_of(((2 * g + 1 - c + i) % 4) * QUARTER, 128), QUARTER)
        return remote(pts.at[:, quarter], both.at[c, :, quarter], sib_s.at[i], sib_r.at[i], sibling)

    def relay(way, j):
        to = device_of(up if way else down, c, g)
        return remote(
            xr.at[way, :, part(j)], fb.at[way, 1 - g, :, part(j)], yr_s.at[way, j], f_r.at[way, 1 - g, j], to
        )

    for j in range(CHUNKS):
        for k in (0, 1):
            x_copy(k, j).start()
            yo_copy(k, j).start()
        sib_copy(j).start()

    loads[1].wait()
    loads[4].wait()
    slot = lax.broadcasted_iota(jnp.int32, (PTS, PTS), 1)
    row = lax.broadcasted_iota(jnp.int32, (PTS, PTS), 0)
    hit = (jnp.broadcast_to(ci_v[...], (PTS, PTS)) == row) & (slot < cc_v[0])
    live = jnp.max(jnp.where(hit, 1.0, 0.0).T, axis=0, keepdims=True)
    loads[0].wait()
    square = jnp.zeros((PTS, PTS), jnp.float32)
    for i in range(D // PTS):
        x = both[c, :, i * PTS : (i + 1) * PTS]
        square = square + x * x
    norm = jnp.sum(square.T, axis=0, keepdims=True)
    info[0] = jnp.broadcast_to(jnp.where(live > 0.5, norm, DEAD), (8, PTS))
    info_to = [(sibling, 1)]
    info_to += [(device_of(q, k, 1 - g), 2 + c) for k in (0, 1)]
    info_to += [(device_of(ahead, k, h), 6 - 2 * c + g) for k in (0, 1) for h in (0, 1)]
    info_to += [(device_of(behind, c, h), 8 + g) for h in (0, 1)]
    info_sends = [
        remote(info.at[0], info.at[s], info_s.at[i], info_r.at[s], to) for i, (to, s) in enumerate(info_to)
    ]
    for send in info_sends:
        send.start()
    loads[2].wait()
    loads[3].wait()
    nb_t[...] = to_lanes(nb_v[...].astype(jnp.float32)).astype(jnp.int32)
    old_t = to_lanes(old_v[...])

    def block_of(s):
        odd = s % 2
        far_pair = jnp.where(s < 8, 4 * up + odd, 4 * ahead + 2 * c + odd)
        far_pair = jnp.where(s < 6, 4 * down + 2 + odd, far_pair)
        near = jnp.where(s == 0, 4 * q + 2 * c + g, 4 * q + 2 * (1 - c) + g)
        near = jnp.where(s < 2, near, 4 * q + 2 * odd + 1 - g)
        return jnp.where(s < 4, near, far_pair)

    def set_bias(s):
        first = block_of(s) * PTS
        ids = first + lax.broadcasted_iota(jnp.int32, (PTS, PTS), 0)
        own_ids = (4 * q + 2 * c + g) * PTS + lax.broadcasted_iota(jnp.int32, (PTS, PTS), 1)
        masked = ids == own_ids
        for k in range(KNN):
            masked = masked | (ids == nb_t[k : k + 1, :])
        key = jnp.broadcast_to(info[s, 0:1, :], (PTS, PTS)).T
        bias[s] = jnp.where(masked, DEAD, key + norm)

    set_bias(0)
    for ref in (gx, gf, gb):
        ref[...] = jnp.zeros_like(ref)
    tiles[0] = jnp.zeros((PTS, PTS), jnp.float32)
    tiles[1] = jnp.zeros((PTS, PTS), jnp.float32)

    def near_blocks(core, j):
        return jnp.concatenate([both[core, :, cols(2 * g + c, j)], xr[core, :, part(j)]], axis=0)

    def far_products(j):
        for way in (0, 1):
            for h in (0, 1):
                remote(
                    xr.at[way, :, part(j)], fb.at[way, h, :, part(j)], yr_s.at[way, j], f_r.at[way, h, j], sibling
                ).wait_recv()
        v0 = near_blocks(0, j)
        f = fb[1, :, :, part(j)].reshape(2 * PTS, WIDTH)
        gf[0] += dot_nt(f, v0)
        b = fb[0, :, :, part(j)].reshape(2 * PTS, WIDTH)
        gb[...] += dot_nt(b, v0)
        gf[1] += dot_nt(f, near_blocks(1, j))

    def far_quarter(j):
        sib_copy(j).wait_recv()
        quarter = pl.ds(pl.multiple_of(((2 * g + c + j) % 4) * QUARTER, 128), QUARTER)
        mine = both[c, :, quarter]
        tiles[0] += dot_nt(mine, mine)
        tiles[1] += dot_nt(both[1 - c, :, quarter], mine)

    gx_copy = remote(gx, gx_r, red_s.at[0], red_r.at[0], sibling)
    gf_copy = remote(gf.at[1 - c], gf_r, red_s.at[1], red_r.at[1], sibling)
    gb_copy = remote(gb, gb_r, red_s.at[2], red_r.at[2], sibling)

    for j in range(CHUNKS):
        for way in (0, 1):
            remote(
                pts.at[:, cols(0, 0)], xr.at[way, :, part(j)], x_s.at[0, j], x_r.at[way, j], sibling
            ).wait_recv()
            relay(way, j).start()
        far_quarter(j)
        xs = jnp.concatenate([xr[0, :, part(j)], xr[1, :, part(j)]], axis=0)
        own = jnp.concatenate([both[0, :, cols(2 * g + c, j)], both[1, :, cols(2 * g + c, j)]], axis=0)
        gx[...] += dot_nt(xs, own)
        if j == 0:

            def each(s, carry):
                remote(info.at[0], info.at[s], info_s.at[0], info_r.at[s], sibling).wait_recv()
                set_bias(s)
                return carry

            lax.fori_loop(1, 10, each, 0)
        if j == CHUNKS - 1:
            gx_copy.start()
        if j > 0:
            far_products(j - 1)

    gx_copy.wait_recv()
    total = gx[...] + gx_r[...]
    for k in (0, 1):
        hx[k] = total[k * PTS : (k + 1) * PTS]
    other = device_of(q, c, 1 - g)
    rx_copy = remote(hx.at[c], rx, t_s.at[0], rx_sem, other)
    rx_copy.start()

    far_products(CHUNKS - 1)
    gf_copy.start()

    @pl.when(c == 1)
    def _():
        gb_copy.start()

    gf_copy.wait_recv()
    total = gf[c] + gf_r[...]
    for rel in (0, 1):
        hf[rel] = total[:, rel * PTS : (rel + 1) * PTS]
    rv_copy = remote(hf.at[1], rv, t_s.at[1], rv_sem, other)
    rv_copy.start()

    def ru_copy(src, half_slot, rel, h, sem, to):
        name = g if rel == 0 else 1 - g
        return remote(
            src.at[rel, pl.ds(h * PTS, PTS)], ru.at[g, half_slot, name], sem, ru_sem.at[g, half_slot, name], to
        )

    fu_copies = [
        ru_copy(hf, c, rel, h, t_s.at[2 + 2 * rel + h], device_of(down, 1, h)) for rel in (0, 1) for h in (0, 1)
    ]
    for copy in fu_copies:
        copy.start()
    rbv_copy = remote(hb.at[1], rbv, t_s.at[6], rbv_sem, device_of(q, 0, 1 - g))
    bu_copies = [
        ru_copy(hb, 1, rel, h, t_s.at[7 + 2 * rel + h], device_of(up, 0, h)) for rel in (0, 1) for h in (0, 1)
    ]

    @pl.when(c == 0)
    def _():
        gb_copy.wait_recv()
        for rel in (0, 1):
            half = pl.ds(rel * PTS, PTS)
            hb[rel] = gb[:, half] + gb_r[:, half]
        rbv_copy.start()
        for copy in bu_copies:
            copy.start()

    def taken(best, s, inner):
        value = bias[s]
        dist = jnp.where(value >= 1e34, FAR, (value - 2.0 * inner) / D)
        return merge_lists(best, sort_lists([dist[8 * i : 8 * i + 8] for i in range(KNN)]))

    low, high = jnp.minimum(old_t[:8], old_t[8:]), jnp.maximum(old_t[:8], old_t[8:])
    best = [low, high] + [jnp.full((8, PTS), FAR, jnp.float32)] * (KNN - 2)
    best = taken(best, 0, tiles[0])
    best = taken(best, 1, tiles[1])
    rx_copy.wait_recv()
    lanes = pl.ds(pl.multiple_of(c * PTS, PTS), PTS)
    for k in (0, 1):
        best = taken(best, 2 + k, hx[k, :, lanes] + rx[:, k * PTS : (k + 1) * PTS].T)
    rv_copy.wait_recv()
    for h in (0, 1):
        best = taken(best, 4 + h, hf[0, h * PTS : (h + 1) * PTS] + rv[h * PTS : (h + 1) * PTS])

    def wait_ru(half_slot):
        for half in (0, 1):
            for name in (0, 1):
                remote(
                    hf.at[0, pl.ds(0, PTS)], ru.at[half, half_slot, name], t_s.at[2], ru_sem.at[half, half_slot, name],
                    sibling,
                ).wait_recv()

    @pl.when(c == 0)
    def _():
        rbv_copy.wait_recv()
        for h in (0, 1):
            tiles[2 + h] = hb[0, h * PTS : (h + 1) * PTS] + rbv[h * PTS : (h + 1) * PTS]

    @pl.when(c == 1)
    def _():
        wait_ru(0)
        for h in (0, 1):
            tiles[2 + h] = (ru[0, 0, h] + ru[1, 0, h]).T

    for h in (0, 1):
        best = taken(best, 6 + h, tiles[2 + h])
    wait_ru(1)
    for h in (0, 1):
        best = taken(best, 8 + h, (ru[0, 1, h] + ru[1, 1, h]).T)
    for shift in (4, 2, 1):
        best = merge_lists(best, [pltpu.roll(v, shift, 0) for v in best])

    running = best[KNN - 1]
    first = 0
    for phase, row_peers in enumerate(sum_peers):
        sum_src[phase] = running
        copies = [
            remote(sum_src.at[phase], sum_in.at[first + i], sum_s.at[first + i], sum_r.at[first + i], peer)
            for i, peer in enumerate(row_peers)
        ]
        for copy in copies:
            copy.start()
        for copy in copies:
            copy.wait_recv()
        for i in range(len(copies)):
            running = running + sum_in[first + i]
        for copy in copies:
            copy.wait_send()
        first += len(copies)
    mean = jnp.sum(running[0:1, :], axis=1, keepdims=True) / (PTS * NODES * 4)
    for k in range(KNN):
        out[k : k + 1, :] = best[k][0:1, :] / mean

    for j in range(CHUNKS):
        for k in (0, 1):
            x_copy(k, j).wait_send()
            yo_copy(k, j).wait_send()
            relay(k, j).wait_send()
        sib_copy(j).wait_send()
    for send in info_sends:
        send.wait_send()
    for copy in [gx_copy, gf_copy, rx_copy, rv_copy, *fu_copies]:
        copy.wait_send()

    @pl.when(c == 1)
    def _():
        gb_copy.wait_send()

    @pl.when(c == 0)
    def _():
        rbv_copy.wait_send()
        for copy in bu_copies:
            copy.wait_send()


def body(points, cand_index, cand_count, neighbor_ids, old_dist):
    f32, dma = jnp.float32, pltpu.SemaphoreType.DMA
    n_sum = sum(len(row) for row in ([0] * 7, [0] * 3, [0] * 7))
    vmem = pltpu.VMEM
    any_spec = pl.BlockSpec(memory_space=pl.ANY)
    scratch = [
        vmem((2, PTS, D), f32),
        vmem((2, PTS, QUARTER), f32),
        vmem((2, 2, PTS, QUARTER), f32),
        vmem((256, 256), f32),
        vmem((2, 256, 256), f32),
        vmem((256, 256), f32),
        vmem((256, 256), f32),
        vmem((256, 256), f32),
        vmem((256, 256), f32),
        vmem((2, 128, 256), f32),
        vmem((2, 256, 128), f32),
        vmem((2, 256, 128), f32),
        vmem((128, 256), f32),
        vmem((256, 128), f32),
        vmem((256, 128), f32),
        vmem((2, 2, 2, 128, 128), f32),
        vmem((10, 8, 128), f32),
        vmem((10, 128, 128), f32),
        vmem((4, 128, 128), f32),
        vmem((128, 16), jnp.int32),
        vmem((128, 16), f32),
        vmem((1, 128), jnp.int32),
        vmem((16, 128), jnp.int32),
        vmem((3, 8, 128), f32),
        vmem((n_sum, 8, 128), f32),
        dma((5,)),
        pltpu.SMEM((1,), jnp.int32),
        dma((CHUNKS,)),
        dma((CHUNKS,)),
        dma((2, CHUNKS)),
        dma((2, CHUNKS)),
        dma((2, CHUNKS)),
        dma((2, CHUNKS)),
        dma((2, 2, CHUNKS)),
        dma((9,)),
        dma((10,)),
        dma((3,)),
        dma((3,)),
        dma((11,)),
        dma,
        dma,
        dma,
        dma((2, 2, 2)),
        dma((n_sum,)),
        dma((n_sum,)),
    ]
    best = pl.pallas_call(
        kernel,
        out_shape=jax.ShapeDtypeStruct((KNN, PTS), f32),
        in_specs=[any_spec] * 5,
        out_specs=pl.BlockSpec(memory_space=pltpu.VMEM),
        scratch_shapes=scratch,
        compiler_params=pltpu.CompilerParams(
            collective_id=0, has_side_effects=True, vmem_limit_bytes=40 << 20
        ),
    )(points, cand_index, cand_count, neighbor_ids, old_dist)
    return best.T


def solution(mesh):
    finer = Mesh(mesh.devices.reshape(*SIZES), AXES)
    return jax.shard_map(
        body,
        mesh=finer,
        in_specs=(P(AXES, None), P(AXES, None), P(AXES), P(AXES, None), P(AXES, None)),
        out_specs=P(AXES, None),
        check_vma=False,
    )
```

```python
import functools

import jax
import jax.numpy as jnp
from jax import lax
from jax.experimental import pallas as pl
from jax.experimental.pallas import tpu as pltpu
from jax.sharding import Mesh
from jax.sharding import PartitionSpec as P

AXES = ("xl", "z", "y", "core", "grp")
SIZES = (2, 8, 4, 2, 2)
NODES = 64
MESH = pl.DeviceIdType.MESH
HIGHEST = lax.Precision.HIGHEST
PTS = 128
D = 4096
KNN = 16
QUARTER = 1024
CHUNKS = 4
WIDTH = QUARTER // CHUNKS
FAR = 1e30
DEAD = 1e35
SUM_PHASES = ((3,), (0, 4, 2), (1,))


def sort_pairs(n):
    pairs = []
    p = 1
    while p < n:
        k = p
        while k >= 1:
            for j in range(k % p, n - k, 2 * k):
                for i in range(min(k, n - j - k)):
                    if (i + j) // (2 * p) == (i + j + k) // (2 * p):
                        pairs.append((i + j, i + j + k))
            k //= 2
        p *= 2
    return pairs


SORT16 = sort_pairs(KNN)


def sort_lists(values):
    values = list(values)
    for i, j in SORT16:
        low, high = jnp.minimum(values[i], values[j]), jnp.maximum(values[i], values[j])
        values[i], values[j] = low, high
    return values


def merge_lists(a, b):
    m = [jnp.minimum(a[i], b[KNN - 1 - i]) for i in range(KNN)]
    step = KNN // 2
    while step:
        for i in range(KNN):
            if not i & step:
                low, high = jnp.minimum(m[i], m[i + step]), jnp.maximum(m[i], m[i + step])
                m[i], m[i + step] = low, high
        step //= 2
    return m


def dot_nt(a, b):
    return lax.dot_general(
        a, b, (((1,), (1,)), ((), ())), precision=HIGHEST, preferred_element_type=jnp.float32
    )


def device_of(node, core, grp):
    return (node // 32, (node // 4) % 8, node % 4, core, grp)


def kernel(
    pts, cidx, ccnt, nbr, old, out,
    both, xr, fb, gx, gf, gb, gx_r, gf_r, gb_r, hx, hf, hb, rx, rv, rbv, ru,
    info, bias, tiles, nb_v, old_v, ci_v, nb_t, sum_src, sum_in,
    loc_sem, cc_v, sib_s, sib_r, x_s, x_r, yo_s, yr_s, f_r, info_s, info_r, red_s, red_r,
    t_s, rx_sem, rv_sem, rbv_sem, ru_sem, sum_s, sum_r,
):
    d = tuple(lax.axis_index(a) for a in AXES)
    c, g = d[3], d[4]
    q = d[0] * 32 + d[1] * 4 + d[2]
    up, down = (q + 1) % NODES, (q + NODES - 1) % NODES
    ahead = (q + NODES + 2 * c - 1) % NODES
    behind = (q + NODES + 1 - 2 * c) % NODES
    sibling = device_of(q, 1 - c, g)
    turned = d[0]

    def turn(bit, by):
        return bit + by - 2 * bit * by

    def quarter_at(core, grp):
        return 2 * turn(grp, core * turned) + core

    def same_quarter(node, core, grp):
        return device_of(node, core, turn(grp, core * turn(turned, node // 32)))

    mine_at = quarter_at(c, g)

    def remote(src, dst, send, recv, to):
        return pltpu.make_async_remote_copy(
            src_ref=src, dst_ref=dst, send_sem=send, recv_sem=recv, device_id=to, device_id_type=MESH
        )

    barrier = pltpu.get_barrier_semaphore()
    peers = [device_of(n, k, h) for n in (up, down) for k in (0, 1) for h in (0, 1)]
    peers.append(device_of(q, 1 - c, 1 - g))
    sum_peers = []
    for axes in SUM_PHASES:
        count = 1
        for a in axes:
            count *= SIZES[a]
        row = []
        for offset in range(1, count):
            at, rest = list(d), offset
            for a in axes:
                at[a] = (d[a] + rest % SIZES[a]) % SIZES[a]
                rest //= SIZES[a]
            row.append(tuple(at))
        sum_peers.append(row)
        peers += row
    for peer in peers:
        pl.semaphore_signal(barrier, inc=1, device_id=peer, device_id_type=MESH)
    loads = [
        pltpu.make_async_copy(pts, both.at[c], loc_sem.at[0]),
        pltpu.make_async_copy(cidx, ci_v, loc_sem.at[1]),
        pltpu.make_async_copy(nbr, nb_v, loc_sem.at[2]),
        pltpu.make_async_copy(old, old_v, loc_sem.at[3]),
        pltpu.make_async_copy(ccnt, cc_v, loc_sem.at[4]),
    ]
    for load in loads:
        load.start()
    pl.semaphore_wait(barrier, len(peers))

    def cols(quarter, j):
        return pl.ds(pl.multiple_of(quarter * QUARTER + j * WIDTH, 128), WIDTH)

    def part(j):
        return pl.ds(j * WIDTH, WIDTH)

    def x_copy(k, j):
        return remote(
            pts.at[:, cols(quarter_at(k, 1 - g), j)], xr.at[c, :, part(j)], x_s.at[k, j], x_r.at[c, j],
            device_of(q, k, 1 - g),
        )

    def yo_copy(k, j):
        return remote(
            pts.at[:, cols(quarter_at(k, g), j)], fb.at[c, g, :, part(j)], yo_s.at[k, j], f_r.at[c, g, j],
            same_quarter(ahead, k, g),
        )

    def sib_copy(i):
        quarter = pl.ds(pl.multiple_of(((quarter_at(1 - c, g) + i) % 4) * QUARTER, 128), QUARTER)
        return remote(pts.at[:, quarter], both.at[c, :, quarter], sib_s.at[i], sib_r.at[i], sibling)

    def relay(way, j):
        to = same_quarter(up if way else down, c, g)
        return remote(
            xr.at[way, :, part(j)], fb.at[way, 1 - g, :, part(j)], yr_s.at[way, j], f_r.at[way, 1 - g, j], to
        )

    for j in range(CHUNKS):
        for k in (0, 1):
            x_copy(k, j).start()
            yo_copy(k, j).start()
        sib_copy(j).start()

    loads[1].wait()
    loads[4].wait()
    slot = lax.broadcasted_iota(jnp.int32, (PTS, PTS), 1)
    row = lax.broadcasted_iota(jnp.int32, (PTS, PTS), 0)
    hit = (jnp.broadcast_to(ci_v[...], (PTS, PTS)) == row) & (slot < cc_v[0])
    live = jnp.max(jnp.where(hit, 1.0, 0.0).T, axis=0, keepdims=True)
    loads[0].wait()
    square = jnp.zeros((PTS, PTS), jnp.float32)
    for i in range(D // PTS):
        x = both[c, :, i * PTS : (i + 1) * PTS]
        square = square + x * x
    norm = jnp.sum(square.T, axis=0, keepdims=True)
    info[0] = jnp.broadcast_to(jnp.where(live > 0.5, norm, DEAD), (8, PTS))
    info_to = [(sibling, 1)]
    info_to += [(device_of(q, k, 1 - g), 2 + c) for k in (0, 1)]
    info_to += [(device_of(ahead, k, h), 6 - 2 * c + g) for k in (0, 1) for h in (0, 1)]
    info_to += [(device_of(behind, c, h), 8 + g) for h in (0, 1)]
    info_sends = [
        remote(info.at[0], info.at[s], info_s.at[i], info_r.at[s], to) for i, (to, s) in enumerate(info_to)
    ]
    for send in info_sends:
        send.start()
    loads[2].wait()
    loads[3].wait()
    nb_t[...] = nb_v[...]
    old_t = old_v[...]

    def block_of(s):
        odd = s % 2
        far_pair = jnp.where(s < 8, 4 * up + odd, 4 * ahead + 2 * c + odd)
        far_pair = jnp.where(s < 6, 4 * down + 2 + odd, far_pair)
        near = jnp.where(s == 0, 4 * q + 2 * c + g, 4 * q + 2 * (1 - c) + g)
        near = jnp.where(s < 2, near, 4 * q + 2 * odd + 1 - g)
        return jnp.where(s < 4, near, far_pair)

    def set_bias(s):
        first = block_of(s) * PTS
        ids = first + lax.broadcasted_iota(jnp.int32, (PTS, PTS), 0)
        own_ids = (4 * q + 2 * c + g) * PTS + lax.broadcasted_iota(jnp.int32, (PTS, PTS), 1)
        masked = ids == own_ids
        for k in range(KNN):
            masked = masked | (ids == nb_t[k : k + 1, :])
        key = jnp.broadcast_to(info[s, 0:1, :], (PTS, PTS)).T
        bias[s] = jnp.where(masked, DEAD, key + norm)

    set_bias(0)
    for ref in (gx, gf, gb):
        ref[...] = jnp.zeros_like(ref)
    tiles[0] = jnp.zeros((PTS, PTS), jnp.float32)
    tiles[1] = jnp.zeros((PTS, PTS), jnp.float32)

    def near_blocks(core, j):
        return jnp.concatenate([both[core, :, cols(mine_at, j)], xr[core, :, part(j)]], axis=0)

    def far_products(j):
        for way in (0, 1):
            for h in (0, 1):
                remote(
                    xr.at[way, :, part(j)], fb.at[way, h, :, part(j)], yr_s.at[way, j], f_r.at[way, h, j], sibling
                ).wait_recv()
        v0 = near_blocks(0, j)
        f = fb[1, :, :, part(j)].reshape(2 * PTS, WIDTH)
        gf[0] += dot_nt(f, v0)
        b = fb[0, :, :, part(j)].reshape(2 * PTS, WIDTH)
        gb[...] += dot_nt(b, v0)
        gf[1] += dot_nt(f, near_blocks(1, j))

    def far_quarter(j):
        sib_copy(j).wait_recv()
        quarter = pl.ds(pl.multiple_of(((mine_at + j) % 4) * QUARTER, 128), QUARTER)
        mine = both[c, :, quarter]
        tiles[0] += dot_nt(mine, mine)
        tiles[1] += dot_nt(both[1 - c, :, quarter], mine)

    gx_copy = remote(gx, gx_r, red_s.at[0], red_r.at[0], sibling)
    gf_copy = remote(gf.at[1 - c], gf_r, red_s.at[1], red_r.at[1], sibling)
    gb_copy = remote(gb, gb_r, red_s.at[2], red_r.at[2], sibling)

    for j in range(CHUNKS):
        for way in (0, 1):
            remote(
                pts.at[:, cols(0, 0)], xr.at[way, :, part(j)], x_s.at[0, j], x_r.at[way, j], sibling
            ).wait_recv()
            relay(way, j).start()
        far_quarter(j)
        xs = jnp.concatenate([xr[0, :, part(j)], xr[1, :, part(j)]], axis=0)
        own = jnp.concatenate([both[0, :, cols(mine_at, j)], both[1, :, cols(mine_at, j)]], axis=0)
        gx[...] += dot_nt(xs, own)
        if j == CHUNKS - 1:
            gx_copy.start()
        if j > 0:
            far_products(j - 1)

    gx_copy.wait_recv()
    total = gx[...] + gx_r[...]
    for k in (0, 1):
        hx[k] = total[k * PTS : (k + 1) * PTS]
    other = device_of(q, c, 1 - g)
    rx_copy = remote(hx.at[c], rx, t_s.at[0], rx_sem, other)
    rx_copy.start()

    def each(s, carry):
        remote(info.at[0], info.at[s], info_s.at[0], info_r.at[s], sibling).wait_recv()
        set_bias(s)
        return carry

    lax.fori_loop(1, 10, each, 0)
    far_products(CHUNKS - 1)
    gf_copy.start()

    @pl.when(c == 1)
    def _():
        gb_copy.start()

    gf_copy.wait_recv()
    total = gf[c] + gf_r[...]
    for rel in (0, 1):
        hf[rel] = total[:, rel * PTS : (rel + 1) * PTS]
    rv_copy = remote(hf.at[1], rv, t_s.at[1], rv_sem, other)
    rv_copy.start()

    def ru_copy(src, half_slot, rel, h, sem, to):
        name = g if rel == 0 else 1 - g
        return remote(
            src.at[rel, pl.ds(h * PTS, PTS)], ru.at[g, half_slot, name], sem, ru_sem.at[g, half_slot, name], to
        )

    fu_copies = [
        ru_copy(hf, c, rel, h, t_s.at[2 + 2 * rel + h], device_of(down, 1, h)) for rel in (0, 1) for h in (0, 1)
    ]
    for copy in fu_copies:
        copy.start()
    rbv_copy = remote(hb.at[1], rbv, t_s.at[6], rbv_sem, device_of(q, 0, 1 - g))
    bu_copies = [
        ru_copy(hb, 1, rel, h, t_s.at[7 + 2 * rel + h], device_of(up, 0, h)) for rel in (0, 1) for h in (0, 1)
    ]

    @pl.when(c == 0)
    def _():
        gb_copy.wait_recv()
        for rel in (0, 1):
            half = pl.ds(rel * PTS, PTS)
            hb[rel] = gb[:, half] + gb_r[:, half]
        rbv_copy.start()
        for copy in bu_copies:
            copy.start()

    def taken(best, s, inner):
        value = bias[s]
        dist = jnp.where(value >= 1e34, FAR, (value - 2.0 * inner) / D)
        return merge_lists(best, sort_lists([dist[8 * i : 8 * i + 8] for i in range(KNN)]))

    low, high = jnp.minimum(old_t[:8], old_t[8:]), jnp.maximum(old_t[:8], old_t[8:])
    best = [low, high] + [jnp.full((8, PTS), FAR, jnp.float32)] * (KNN - 2)
    best = taken(best, 0, tiles[0])
    best = taken(best, 1, tiles[1])
    rx_copy.wait_recv()
    lanes = pl.ds(pl.multiple_of(c * PTS, PTS), PTS)
    for k in (0, 1):
        best = taken(best, 2 + k, hx[k, :, lanes] + rx[:, k * PTS : (k + 1) * PTS].T)
    rv_copy.wait_recv()
    for h in (0, 1):
        best = taken(best, 4 + h, hf[0, h * PTS : (h + 1) * PTS] + rv[h * PTS : (h + 1) * PTS])

    def wait_ru(half_slot):
        for half in (0, 1):
            for name in (0, 1):
                remote(
                    hf.at[0, pl.ds(0, PTS)], ru.at[half, half_slot, name], t_s.at[2], ru_sem.at[half, half_slot, name],
                    sibling,
                ).wait_recv()

    @pl.when(c == 0)
    def _():
        rbv_copy.wait_recv()
        for h in (0, 1):
            tiles[2 + h] = hb[0, h * PTS : (h + 1) * PTS] + rbv[h * PTS : (h + 1) * PTS]

    @pl.when(c == 1)
    def _():
        wait_ru(0)
        for h in (0, 1):
            tiles[2 + h] = (ru[0, 0, h] + ru[1, 0, h]).T

    for h in (0, 1):
        best = taken(best, 6 + h, tiles[2 + h])
    wait_ru(1)
    for h in (0, 1):
        best = taken(best, 8 + h, (ru[0, 1, h] + ru[1, 1, h]).T)
    for shift in (4, 2, 1):
        best = merge_lists(best, [pltpu.roll(v, shift, 0) for v in best])

    running = best[KNN - 1][0:1, :]
    sum_copies = []
    first = 0
    for phase, row_peers in enumerate(sum_peers):
        sum_src[phase] = running
        copies = [
            remote(sum_src.at[phase], sum_in.at[first + i], sum_s.at[first + i], sum_r.at[first + i], peer)
            for i, peer in enumerate(row_peers)
        ]
        for copy in copies:
            copy.start()
        for copy in copies:
            copy.wait_recv()
        for i in range(len(copies)):
            running = running + sum_in[first + i]
        sum_copies += copies
        first += len(copies)
    mean = jnp.sum(running, axis=1, keepdims=True) / (PTS * NODES * 4)
    for k in range(KNN):
        out[k : k + 1, :] = best[k][0:1, :] / mean

    for j in range(CHUNKS):
        for k in (0, 1):
            x_copy(k, j).wait_send()
            yo_copy(k, j).wait_send()
            relay(k, j).wait_send()
        sib_copy(j).wait_send()
    for send in info_sends:
        send.wait_send()
    for copy in [gx_copy, gf_copy, rx_copy, rv_copy, *fu_copies, *sum_copies]:
        copy.wait_send()

    @pl.when(c == 1)
    def _():
        gb_copy.wait_send()

    @pl.when(c == 0)
    def _():
        rbv_copy.wait_send()
        for copy in bu_copies:
            copy.wait_send()


def body(points, cand_index, cand_count, neighbor_ids, old_dist):
    f32, dma = jnp.float32, pltpu.SemaphoreType.DMA
    n_sum = 1 + 15 + 7
    vmem = pltpu.VMEM
    any_spec = pl.BlockSpec(memory_space=pltpu.HBM)
    scratch = [
        vmem((2, PTS, D), f32),
        vmem((2, PTS, QUARTER), f32),
        vmem((2, 2, PTS, QUARTER), f32),
        vmem((256, 256), f32),
        vmem((2, 256, 256), f32),
        vmem((256, 256), f32),
        vmem((256, 256), f32),
        vmem((256, 256), f32),
        vmem((256, 256), f32),
        vmem((2, 128, 256), f32),
        vmem((2, 256, 128), f32),
        vmem((2, 256, 128), f32),
        vmem((128, 256), f32),
        vmem((256, 128), f32),
        vmem((256, 128), f32),
        vmem((2, 2, 2, 128, 128), f32),
        vmem((10, 8, 128), f32),
        vmem((10, 128, 128), f32),
        vmem((4, 128, 128), f32),
        vmem((16, 128), jnp.int32),
        vmem((16, 128), f32),
        vmem((1, 128), jnp.int32),
        vmem((16, 128), jnp.int32),
        vmem((3, 1, 128), f32),
        vmem((n_sum, 1, 128), f32),
        dma((5,)),
        pltpu.SMEM((1,), jnp.int32),
        dma((CHUNKS,)),
        dma((CHUNKS,)),
        dma((2, CHUNKS)),
        dma((2, CHUNKS)),
        dma((2, CHUNKS)),
        dma((2, CHUNKS)),
        dma((2, 2, CHUNKS)),
        dma((9,)),
        dma((10,)),
        dma((3,)),
        dma((3,)),
        dma((11,)),
        dma,
        dma,
        dma,
        dma((2, 2, 2)),
        dma((n_sum,)),
        dma((n_sum,)),
    ]
    best = pl.pallas_call(
        kernel,
        out_shape=jax.ShapeDtypeStruct((KNN, PTS), f32),
        in_specs=[any_spec] * 5,
        out_specs=pl.BlockSpec(memory_space=pltpu.VMEM),
        scratch_shapes=scratch,
        compiler_params=pltpu.CompilerParams(
            collective_id=0, has_side_effects=True, vmem_limit_bytes=40 << 20
        ),
    )(points, cand_index, cand_count, neighbor_ids.T, old_dist.T)
    return best.T


def solution(mesh):
    finer = Mesh(mesh.devices.reshape(*SIZES), AXES)
    return jax.shard_map(
        body,
        mesh=finer,
        in_specs=(P(AXES, None), P(AXES, None), P(AXES), P(AXES, None), P(AXES, None)),
        out_specs=P(AXES, None),
        check_vma=False,
    )
```

```python
import functools

import jax
import jax.numpy as jnp
from jax import lax
from jax.experimental import pallas as pl
from jax.experimental.pallas import tpu as pltpu
from jax.sharding import Mesh
from jax.sharding import PartitionSpec as P

AXES = ("xl", "z", "y", "core", "grp")
SIZES = (2, 8, 4, 2, 2)
NODES = 64
MESH = pl.DeviceIdType.MESH
HIGHEST = lax.Precision.HIGHEST
PTS = 128
D = 4096
KNN = 16
QUARTER = 1024
CHUNKS = 4
WIDTH = QUARTER // CHUNKS
FAR = 1e30
DEAD = 1e35
SUM_PHASES = ((3,), (0, 4, 2), (1,))


def sort_pairs(n):
    pairs = []
    p = 1
    while p < n:
        k = p
        while k >= 1:
            for j in range(k % p, n - k, 2 * k):
                for i in range(min(k, n - j - k)):
                    if (i + j) // (2 * p) == (i + j + k) // (2 * p):
                        pairs.append((i + j, i + j + k))
            k //= 2
        p *= 2
    return pairs


SORT16 = sort_pairs(KNN)


def sort_lists(values):
    values = list(values)
    for i, j in SORT16:
        low, high = jnp.minimum(values[i], values[j]), jnp.maximum(values[i], values[j])
        values[i], values[j] = low, high
    return values


def merge_lists(a, b):
    m = [jnp.minimum(a[i], b[KNN - 1 - i]) for i in range(KNN)]
    step = KNN // 2
    while step:
        for i in range(KNN):
            if not i & step:
                low, high = jnp.minimum(m[i], m[i + step]), jnp.maximum(m[i], m[i + step])
                m[i], m[i + step] = low, high
        step //= 2
    return m


def dot_nt(a, b):
    return lax.dot_general(
        a, b, (((1,), (1,)), ((), ())), precision=HIGHEST, preferred_element_type=jnp.float32
    )


def device_of(node, core, grp):
    return (node // 32, (node // 4) % 8, node % 4, core, grp)


def kernel(
    pts, cidx, ccnt, nbr, old, out,
    both, xr, fb, gx, gf, gb, gx_r, gf_r, gb_r, hx, hf, hb, rx, rv, rbv, ru,
    info, bias, tiles, nb_v, old_v, ci_v, nb_t, sum_src, sum_in,
    loc_sem, cc_v, sib_s, sib_r, x_s, x_r, yo_s, yr_s, f_r, info_s, info_r, red_s, red_r,
    via, via_s, via_r, t_s, rx_sem, rv_sem, rbv_sem, ru_sem, sum_s, sum_r,
):
    d = tuple(lax.axis_index(a) for a in AXES)
    c, g = d[3], d[4]
    q = d[0] * 32 + d[1] * 4 + d[2]
    up, down = (q + 1) % NODES, (q + NODES - 1) % NODES
    ahead = (q + NODES + 2 * c - 1) % NODES
    behind = (q + NODES + 1 - 2 * c) % NODES
    sibling = device_of(q, 1 - c, g)
    turned = d[0]

    def turn(bit, by):
        return bit + by - 2 * bit * by

    def quarter_at(core, grp):
        return 2 * turn(grp, core * turned) + core

    def same_quarter(node, core, grp):
        return device_of(node, core, turn(grp, core * turn(turned, node // 32)))

    mine_at = quarter_at(c, g)

    def remote(src, dst, send, recv, to):
        return pltpu.make_async_remote_copy(
            src_ref=src, dst_ref=dst, send_sem=send, recv_sem=recv, device_id=to, device_id_type=MESH
        )

    barrier = pltpu.get_barrier_semaphore()
    peers = [device_of(n, k, h) for n in (up, down) for k in (0, 1) for h in (0, 1)]
    peers.append(device_of(q, 1 - c, 1 - g))
    sum_peers = []
    for axes in SUM_PHASES:
        count = 1
        for a in axes:
            count *= SIZES[a]
        row = []
        for offset in range(1, count):
            at, rest = list(d), offset
            for a in axes:
                at[a] = (d[a] + rest % SIZES[a]) % SIZES[a]
                rest //= SIZES[a]
            row.append(tuple(at))
        sum_peers.append(row)
        peers += row
    ring = q % 32
    steps = ((c == 1) & (ring == 31)) | ((c == 0) & (ring == 0))
    passes = (ring == 28) | (ring == 3)
    receives = (ring == 0) | (ring == 31)
    onward = ring // 28
    middle = q + 3 - 6 * c
    source = device_of(q - 3 + 6 * onward, onward, g)
    after_node = (1 - d[0]) * 32 + 31 * (1 - onward)
    before_node = (1 - d[0]) * 32 + jnp.where(ring == 0, 28, 3)
    onward_to = same_quarter(after_node, c, g)

    def greet(peer):
        pl.semaphore_signal(barrier, inc=1, device_id=peer, device_id_type=MESH)

    for peer in peers:
        greet(peer)

    @pl.when(steps)
    def _():
        for k in (0, 1):
            greet(device_of(middle, k, g))

    @pl.when(passes)
    def _():
        greet(source)
        greet(onward_to)

    @pl.when(receives)
    def _():
        greet(same_quarter(before_node, c, g))

    greeted = len(peers) + jnp.where(steps, 2, 0) + jnp.where(passes, 2, 0) + jnp.where(receives, 1, 0)
    loads = [
        pltpu.make_async_copy(pts, both.at[c], loc_sem.at[0]),
        pltpu.make_async_copy(cidx, ci_v, loc_sem.at[1]),
        pltpu.make_async_copy(nbr, nb_v, loc_sem.at[2]),
        pltpu.make_async_copy(old, old_v, loc_sem.at[3]),
        pltpu.make_async_copy(ccnt, cc_v, loc_sem.at[4]),
    ]
    for load in loads:
        load.start()
    pl.semaphore_wait(barrier, greeted)

    def cols(quarter, j):
        return pl.ds(pl.multiple_of(quarter * QUARTER + j * WIDTH, 128), WIDTH)

    def part(j):
        return pl.ds(j * WIDTH, WIDTH)

    def x_copy(k, j):
        return remote(
            pts.at[:, cols(quarter_at(k, 1 - g), j)], xr.at[c, :, part(j)], x_s.at[k, j], x_r.at[c, j],
            device_of(q, k, 1 - g),
        )

    def yo_copy(k, j):
        return remote(
            pts.at[:, cols(quarter_at(k, g), j)], fb.at[c, g, :, part(j)], yo_s.at[k, j], f_r.at[c, g, j],
            same_quarter(ahead, k, g),
        )

    def to_middle(k, j):
        return remote(
            pts.at[:, cols(quarter_at(k, g), j)], via.at[:, part(j)], yo_s.at[k, j], via_r.at[j],
            device_of(middle, k, g),
        )

    def pass_on(j):
        return remote(
            via.at[:, part(j)], fb.at[onward, g, :, part(j)], via_s.at[j], f_r.at[onward, g, j], onward_to
        )

    def sib_copy(i):
        quarter = pl.ds(pl.multiple_of(((quarter_at(1 - c, g) + i) % 4) * QUARTER, 128), QUARTER)
        return remote(pts.at[:, quarter], both.at[c, :, quarter], sib_s.at[i], sib_r.at[i], sibling)

    def relay(way, j):
        to = same_quarter(up if way else down, c, g)
        return remote(
            xr.at[way, :, part(j)], fb.at[way, 1 - g, :, part(j)], yr_s.at[way, j], f_r.at[way, 1 - g, j], to
        )

    for j in range(CHUNKS):
        for k in (0, 1):
            x_copy(k, j).start()

            @pl.when(steps)
            def _(k=k, j=j):
                to_middle(k, j).start()

            @pl.when(jnp.logical_not(steps))
            def _(k=k, j=j):
                yo_copy(k, j).start()

        sib_copy(j).start()

    loads[1].wait()
    loads[4].wait()
    slot = lax.broadcasted_iota(jnp.int32, (PTS, PTS), 1)
    row = lax.broadcasted_iota(jnp.int32, (PTS, PTS), 0)
    hit = (jnp.broadcast_to(ci_v[...], (PTS, PTS)) == row) & (slot < cc_v[0])
    live = jnp.max(jnp.where(hit, 1.0, 0.0).T, axis=0, keepdims=True)
    loads[0].wait()
    square = jnp.zeros((PTS, PTS), jnp.float32)
    for i in range(D // PTS):
        x = both[c, :, i * PTS : (i + 1) * PTS]
        square = square + x * x
    norm = jnp.sum(square.T, axis=0, keepdims=True)
    info[0] = jnp.broadcast_to(jnp.where(live > 0.5, norm, DEAD), (8, PTS))
    info_to = [(sibling, 1)]
    info_to += [(device_of(q, k, 1 - g), 2 + c) for k in (0, 1)]
    info_to += [(device_of(ahead, k, h), 6 - 2 * c + g) for k in (0, 1) for h in (0, 1)]
    info_to += [(device_of(behind, c, h), 8 + g) for h in (0, 1)]
    info_sends = [
        remote(info.at[0], info.at[s], info_s.at[i], info_r.at[s], to) for i, (to, s) in enumerate(info_to)
    ]
    for send in info_sends:
        send.start()
    loads[2].wait()
    loads[3].wait()
    nb_t[...] = nb_v[...]
    old_t = old_v[...]

    def block_of(s):
        odd = s % 2
        far_pair = jnp.where(s < 8, 4 * up + odd, 4 * ahead + 2 * c + odd)
        far_pair = jnp.where(s < 6, 4 * down + 2 + odd, far_pair)
        near = jnp.where(s == 0, 4 * q + 2 * c + g, 4 * q + 2 * (1 - c) + g)
        near = jnp.where(s < 2, near, 4 * q + 2 * odd + 1 - g)
        return jnp.where(s < 4, near, far_pair)

    def set_bias(s):
        first = block_of(s) * PTS
        ids = first + lax.broadcasted_iota(jnp.int32, (PTS, PTS), 0)
        own_ids = (4 * q + 2 * c + g) * PTS + lax.broadcasted_iota(jnp.int32, (PTS, PTS), 1)
        masked = ids == own_ids
        for k in range(KNN):
            masked = masked | (ids == nb_t[k : k + 1, :])
        key = jnp.broadcast_to(info[s, 0:1, :], (PTS, PTS)).T
        bias[s] = jnp.where(masked, DEAD, key + norm)

    set_bias(0)
    for ref in (gx, gf, gb):
        ref[...] = jnp.zeros_like(ref)
    tiles[0] = jnp.zeros((PTS, PTS), jnp.float32)
    tiles[1] = jnp.zeros((PTS, PTS), jnp.float32)

    def near_blocks(core, j):
        return jnp.concatenate([both[core, :, cols(mine_at, j)], xr[core, :, part(j)]], axis=0)

    def far_products(j):
        for way in (0, 1):
            for h in (0, 1):
                remote(
                    xr.at[way, :, part(j)], fb.at[way, h, :, part(j)], yr_s.at[way, j], f_r.at[way, h, j], sibling
                ).wait_recv()
        v0 = near_blocks(0, j)
        f = fb[1, :, :, part(j)].reshape(2 * PTS, WIDTH)
        gf[0] += dot_nt(f, v0)
        b = fb[0, :, :, part(j)].reshape(2 * PTS, WIDTH)
        gb[...] += dot_nt(b, v0)
        gf[1] += dot_nt(f, near_blocks(1, j))

    def far_quarter(j):
        sib_copy(j).wait_recv()
        quarter = pl.ds(pl.multiple_of(((mine_at + j) % 4) * QUARTER, 128), QUARTER)
        mine = both[c, :, quarter]
        tiles[0] += dot_nt(mine, mine)
        tiles[1] += dot_nt(both[1 - c, :, quarter], mine)

    gx_copy = remote(gx, gx_r, red_s.at[0], red_r.at[0], sibling)
    gf_copy = remote(gf.at[1 - c], gf_r, red_s.at[1], red_r.at[1], sibling)
    gb_copy = remote(gb, gb_r, red_s.at[2], red_r.at[2], sibling)

    for j in range(CHUNKS):

        @pl.when(passes)
        def _(j=j):
            to_middle(0, j).wait_recv()
            pass_on(j).start()

        for way in (0, 1):
            remote(
                pts.at[:, cols(0, 0)], xr.at[way, :, part(j)], x_s.at[0, j], x_r.at[way, j], sibling
            ).wait_recv()
            relay(way, j).start()
        far_quarter(j)
        xs = jnp.concatenate([xr[0, :, part(j)], xr[1, :, part(j)]], axis=0)
        own = jnp.concatenate([both[0, :, cols(mine_at, j)], both[1, :, cols(mine_at, j)]], axis=0)
        gx[...] += dot_nt(xs, own)
        if j == CHUNKS - 1:
            gx_copy.start()
        if j > 0:
            far_products(j - 1)

    gx_copy.wait_recv()
    total = gx[...] + gx_r[...]
    for k in (0, 1):
        hx[k] = total[k * PTS : (k + 1) * PTS]
    other = device_of(q, c, 1 - g)
    rx_copy = remote(hx.at[c], rx, t_s.at[0], rx_sem, other)
    rx_copy.start()

    def each(s, carry):
        remote(info.at[0], info.at[s], info_s.at[0], info_r.at[s], sibling).wait_recv()
        set_bias(s)
        return carry

    lax.fori_loop(1, 10, each, 0)
    far_products(CHUNKS - 1)
    gf_copy.start()

    @pl.when(c == 1)
    def _():
        gb_copy.start()

    gf_copy.wait_recv()
    total = gf[c] + gf_r[...]
    for rel in (0, 1):
        hf[rel] = total[:, rel * PTS : (rel + 1) * PTS]
    rv_copy = remote(hf.at[1], rv, t_s.at[1], rv_sem, other)
    rv_copy.start()

    def ru_copy(src, half_slot, rel, h, sem, to):
        name = g if rel == 0 else 1 - g
        return remote(
            src.at[rel, pl.ds(h * PTS, PTS)], ru.at[g, half_slot, name], sem, ru_sem.at[g, half_slot, name], to
        )

    fu_copies = [
        ru_copy(hf, c, rel, h, t_s.at[2 + 2 * rel + h], device_of(down, 1, h)) for rel in (0, 1) for h in (0, 1)
    ]
    for copy in fu_copies:
        copy.start()
    rbv_copy = remote(hb.at[1], rbv, t_s.at[6], rbv_sem, device_of(q, 0, 1 - g))
    bu_copies = [
        ru_copy(hb, 1, rel, h, t_s.at[7 + 2 * rel + h], device_of(up, 0, h)) for rel in (0, 1) for h in (0, 1)
    ]

    @pl.when(c == 0)
    def _():
        gb_copy.wait_recv()
        for rel in (0, 1):
            half = pl.ds(rel * PTS, PTS)
            hb[rel] = gb[:, half] + gb_r[:, half]
        rbv_copy.start()
        for copy in bu_copies:
            copy.start()

    def taken(best, s, inner):
        value = bias[s]
        dist = jnp.where(value >= 1e34, FAR, (value - 2.0 * inner) / D)
        return merge_lists(best, sort_lists([dist[8 * i : 8 * i + 8] for i in range(KNN)]))

    low, high = jnp.minimum(old_t[:8], old_t[8:]), jnp.maximum(old_t[:8], old_t[8:])
    best = [low, high] + [jnp.full((8, PTS), FAR, jnp.float32)] * (KNN - 2)
    best = taken(best, 0, tiles[0])
    best = taken(best, 1, tiles[1])
    rx_copy.wait_recv()
    lanes = pl.ds(pl.multiple_of(c * PTS, PTS), PTS)
    for k in (0, 1):
        best = taken(best, 2 + k, hx[k, :, lanes] + rx[:, k * PTS : (k + 1) * PTS].T)
    rv_copy.wait_recv()
    for h in (0, 1):
        best = taken(best, 4 + h, hf[0, h * PTS : (h + 1) * PTS] + rv[h * PTS : (h + 1) * PTS])

    def wait_ru(half_slot):
        for half in (0, 1):
            for name in (0, 1):
                remote(
                    hf.at[0, pl.ds(0, PTS)], ru.at[half, half_slot, name], t_s.at[2], ru_sem.at[half, half_slot, name],
                    sibling,
                ).wait_recv()

    @pl.when(c == 0)
    def _():
        rbv_copy.wait_recv()
        for h in (0, 1):
            tiles[2 + h] = hb[0, h * PTS : (h + 1) * PTS] + rbv[h * PTS : (h + 1) * PTS]

    @pl.when(c == 1)
    def _():
        wait_ru(0)
        for h in (0, 1):
            tiles[2 + h] = (ru[0, 0, h] + ru[1, 0, h]).T

    for h in (0, 1):
        best = taken(best, 6 + h, tiles[2 + h])
    wait_ru(1)
    for h in (0, 1):
        best = taken(best, 8 + h, (ru[0, 1, h] + ru[1, 1, h]).T)
    for shift in (4, 2, 1):
        best = merge_lists(best, [pltpu.roll(v, shift, 0) for v in best])

    running = best[KNN - 1][0:1, :]
    sum_copies = []
    first = 0
    for phase, row_peers in enumerate(sum_peers):
        sum_src[phase] = running
        copies = [
            remote(sum_src.at[phase], sum_in.at[first + i], sum_s.at[first + i], sum_r.at[first + i], peer)
            for i, peer in enumerate(row_peers)
        ]
        for copy in copies:
            copy.start()
        for copy in copies:
            copy.wait_recv()
        for i in range(len(copies)):
            running = running + sum_in[first + i]
        sum_copies += copies
        first += len(copies)
    mean = jnp.sum(running, axis=1, keepdims=True) / (PTS * NODES * 4)
    for k in range(KNN):
        out[k : k + 1, :] = best[k][0:1, :] / mean

    for j in range(CHUNKS):
        for k in (0, 1):
            x_copy(k, j).wait_send()
            yo_copy(k, j).wait_send()
            relay(k, j).wait_send()
        sib_copy(j).wait_send()

        @pl.when(passes)
        def _(j=j):
            pass_on(j).wait_send()

    for send in info_sends:
        send.wait_send()
    for copy in [gx_copy, gf_copy, rx_copy, rv_copy, *fu_copies, *sum_copies]:
        copy.wait_send()

    @pl.when(c == 1)
    def _():
        gb_copy.wait_send()

    @pl.when(c == 0)
    def _():
        rbv_copy.wait_send()
        for copy in bu_copies:
            copy.wait_send()


def body(points, cand_index, cand_count, neighbor_ids, old_dist):
    f32, dma = jnp.float32, pltpu.SemaphoreType.DMA
    n_sum = 1 + 15 + 7
    vmem = pltpu.VMEM
    any_spec = pl.BlockSpec(memory_space=pltpu.HBM)
    scratch = [
        vmem((2, PTS, D), f32),
        vmem((2, PTS, QUARTER), f32),
        vmem((2, 2, PTS, QUARTER), f32),
        vmem((256, 256), f32),
        vmem((2, 256, 256), f32),
        vmem((256, 256), f32),
        vmem((256, 256), f32),
        vmem((256, 256), f32),
        vmem((256, 256), f32),
        vmem((2, 128, 256), f32),
        vmem((2, 256, 128), f32),
        vmem((2, 256, 128), f32),
        vmem((128, 256), f32),
        vmem((256, 128), f32),
        vmem((256, 128), f32),
        vmem((2, 2, 2, 128, 128), f32),
        vmem((10, 8, 128), f32),
        vmem((10, 128, 128), f32),
        vmem((4, 128, 128), f32),
        vmem((16, 128), jnp.int32),
        vmem((16, 128), f32),
        vmem((1, 128), jnp.int32),
        vmem((16, 128), jnp.int32),
        vmem((3, 1, 128), f32),
        vmem((n_sum, 1, 128), f32),
        dma((5,)),
        pltpu.SMEM((1,), jnp.int32),
        dma((CHUNKS,)),
        dma((CHUNKS,)),
        dma((2, CHUNKS)),
        dma((2, CHUNKS)),
        dma((2, CHUNKS)),
        dma((2, CHUNKS)),
        dma((2, 2, CHUNKS)),
        dma((9,)),
        dma((10,)),
        dma((3,)),
        dma((3,)),
        vmem((PTS, QUARTER), f32),
        dma((CHUNKS,)),
        dma((CHUNKS,)),
        dma((11,)),
        dma,
        dma,
        dma,
        dma((2, 2, 2)),
        dma((n_sum,)),
        dma((n_sum,)),
    ]
    best = pl.pallas_call(
        kernel,
        out_shape=jax.ShapeDtypeStruct((KNN, PTS), f32),
        in_specs=[any_spec] * 5,
        out_specs=pl.BlockSpec(memory_space=pltpu.VMEM),
        scratch_shapes=scratch,
        compiler_params=pltpu.CompilerParams(
            collective_id=0, has_side_effects=True, vmem_limit_bytes=40 << 20
        ),
    )(points, cand_index, cand_count, neighbor_ids.T, old_dist.T)
    return best.T


def solution(mesh):
    finer = Mesh(mesh.devices.reshape(*SIZES), AXES)
    return jax.shard_map(
        body,
        mesh=finer,
        in_specs=(P(AXES, None), P(AXES, None), P(AXES), P(AXES, None), P(AXES, None)),
        out_specs=P(AXES, None),
        check_vma=False,
    )
```

```python
import functools

import jax
import jax.numpy as jnp
from jax import lax
from jax.experimental import pallas as pl
from jax.experimental.pallas import tpu as pltpu
from jax.sharding import Mesh
from jax.sharding import PartitionSpec as P

AXES = ("xl", "z", "y", "core", "grp")
SIZES = (2, 8, 4, 2, 2)
NODES = 64
MESH = pl.DeviceIdType.MESH
HIGHEST = lax.Precision.HIGHEST
PTS = 128
D = 4096
KNN = 16
QUARTER = 1024
CHUNKS = 4
WIDTH = QUARTER // CHUNKS
FAR = 1e30
DEAD = 1e35
SUM_PHASES = ((3,), (0, 4, 2), (1,))


def sort_pairs(n):
    pairs = []
    p = 1
    while p < n:
        k = p
        while k >= 1:
            for j in range(k % p, n - k, 2 * k):
                for i in range(min(k, n - j - k)):
                    if (i + j) // (2 * p) == (i + j + k) // (2 * p):
                        pairs.append((i + j, i + j + k))
            k //= 2
        p *= 2
    return pairs


SORT16 = sort_pairs(KNN)


def sort_lists(values):
    values = list(values)
    for i, j in SORT16:
        low, high = jnp.minimum(values[i], values[j]), jnp.maximum(values[i], values[j])
        values[i], values[j] = low, high
    return values


def merge_lists(a, b):
    m = [jnp.minimum(a[i], b[KNN - 1 - i]) for i in range(KNN)]
    step = KNN // 2
    while step:
        for i in range(KNN):
            if not i & step:
                low, high = jnp.minimum(m[i], m[i + step]), jnp.maximum(m[i], m[i + step])
                m[i], m[i + step] = low, high
        step //= 2
    return m


def dot_nt(a, b):
    return lax.dot_general(
        a, b, (((1,), (1,)), ((), ())), precision=HIGHEST, preferred_element_type=jnp.float32
    )


def device_of(node, core, grp):
    return (node // 32, (node // 4) % 8, node % 4, core, grp)


def kernel(
    pts, cidx, ccnt, nbr, old, out,
    both, xr, fb, gx, gf, gb, gx_r, gf_r, gb_r, hx, hf, hb, rx, rv, rbv, ru,
    info, bias, tiles, nb_v, old_v, ci_v, nb_t, sum_src, sum_in,
    loc_sem, cc_v, sib_s, sib_r, x_s, x_r, yo_s, yr_s, f_r, info_s, info_r, red_s, red_r,
    via, via_s, via_r, t_s, rx_sem, rv_sem, rbv_sem, ru_sem, sum_s, sum_r,
):
    d = tuple(lax.axis_index(a) for a in AXES)
    c, g = d[3], d[4]
    q = d[0] * 32 + d[1] * 4 + d[2]
    up, down = (q + 1) % NODES, (q + NODES - 1) % NODES
    ahead = (q + NODES + 2 * c - 1) % NODES
    behind = (q + NODES + 1 - 2 * c) % NODES
    sibling = device_of(q, 1 - c, g)
    turned = d[0]

    def turn(bit, by):
        return bit + by - 2 * bit * by

    def quarter_at(core, grp):
        return 2 * turn(grp, core * turned) + core

    def same_quarter(node, core, grp):
        return device_of(node, core, turn(grp, core * turn(turned, node // 32)))

    mine_at = quarter_at(c, g)

    def remote(src, dst, send, recv, to):
        return pltpu.make_async_remote_copy(
            src_ref=src, dst_ref=dst, send_sem=send, recv_sem=recv, device_id=to, device_id_type=MESH
        )

    barrier = pltpu.get_barrier_semaphore()
    peers = [device_of(n, k, h) for n in (up, down) for k in (0, 1) for h in (0, 1)]
    peers.append(device_of(q, 1 - c, 1 - g))
    sum_peers = []
    for axes in SUM_PHASES:
        count = 1
        for a in axes:
            count *= SIZES[a]
        row = []
        for offset in range(1, count):
            at, rest = list(d), offset
            for a in axes:
                at[a] = (d[a] + rest % SIZES[a]) % SIZES[a]
                rest //= SIZES[a]
            row.append(tuple(at))
        sum_peers.append(row)
        peers += row
    ring = q % 32
    steps = ((c == 1) & (ring == 31)) | ((c == 0) & (ring == 0))
    passes = (ring == 0) | (ring == 31)
    onward = 1 - ring // 31
    middle = q + 31 - 62 * c
    source = device_of(q - 31 + 62 * onward, onward, g)
    after_node = (1 - d[0]) * 32 + 31 * (1 - onward)
    onward_to = same_quarter(after_node, c, g)

    def greet(peer):
        pl.semaphore_signal(barrier, inc=1, device_id=peer, device_id_type=MESH)

    for peer in peers:
        greet(peer)

    @pl.when(steps)
    def _():
        for k in (0, 1):
            greet(device_of(middle, k, g))

    @pl.when(passes)
    def _():
        greet(source)
        greet(onward_to)

    greeted = len(peers) + jnp.where(steps, 2, 0) + jnp.where(passes, 2, 0)
    loads = [
        pltpu.make_async_copy(pts, both.at[c], loc_sem.at[0]),
        pltpu.make_async_copy(cidx, ci_v, loc_sem.at[1]),
        pltpu.make_async_copy(nbr, nb_v, loc_sem.at[2]),
        pltpu.make_async_copy(old, old_v, loc_sem.at[3]),
        pltpu.make_async_copy(ccnt, cc_v, loc_sem.at[4]),
    ]
    for load in loads:
        load.start()
    pl.semaphore_wait(barrier, greeted)

    def cols(quarter, j):
        return pl.ds(pl.multiple_of(quarter * QUARTER + j * WIDTH, 128), WIDTH)

    def part(j):
        return pl.ds(j * WIDTH, WIDTH)

    def x_copy(k, j):
        return remote(
            pts.at[:, cols(quarter_at(k, 1 - g), j)], xr.at[c, :, part(j)], x_s.at[k, j], x_r.at[c, j],
            device_of(q, k, 1 - g),
        )

    def yo_copy(k, j):
        return remote(
            pts.at[:, cols(quarter_at(k, g), j)], fb.at[c, g, :, part(j)], yo_s.at[k, j], f_r.at[c, g, j],
            same_quarter(ahead, k, g),
        )

    def to_middle(k, j):
        return remote(
            pts.at[:, cols(quarter_at(k, g), j)], via.at[:, part(j)], yo_s.at[k, j], via_r.at[j],
            device_of(middle, k, g),
        )

    def pass_on(j):
        return remote(
            via.at[:, part(j)], fb.at[onward, g, :, part(j)], via_s.at[j], f_r.at[onward, g, j], onward_to
        )

    def sib_copy(i):
        quarter = pl.ds(pl.multiple_of(((quarter_at(1 - c, g) + i) % 4) * QUARTER, 128), QUARTER)
        return remote(pts.at[:, quarter], both.at[c, :, quarter], sib_s.at[i], sib_r.at[i], sibling)

    def relay(way, j):
        to = same_quarter(up if way else down, c, g)
        return remote(
            xr.at[way, :, part(j)], fb.at[way, 1 - g, :, part(j)], yr_s.at[way, j], f_r.at[way, 1 - g, j], to
        )

    for j in range(CHUNKS):
        for k in (0, 1):
            x_copy(k, j).start()

            @pl.when(steps)
            def _(k=k, j=j):
                to_middle(k, j).start()

            @pl.when(jnp.logical_not(steps))
            def _(k=k, j=j):
                yo_copy(k, j).start()

        sib_copy(j).start()

    loads[1].wait()
    loads[4].wait()
    slot = lax.broadcasted_iota(jnp.int32, (PTS, PTS), 1)
    row = lax.broadcasted_iota(jnp.int32, (PTS, PTS), 0)
    hit = (jnp.broadcast_to(ci_v[...], (PTS, PTS)) == row) & (slot < cc_v[0])
    live = jnp.max(jnp.where(hit, 1.0, 0.0).T, axis=0, keepdims=True)
    loads[0].wait()
    square = jnp.zeros((PTS, PTS), jnp.float32)
    for i in range(D // PTS):
        x = both[c, :, i * PTS : (i + 1) * PTS]
        square = square + x * x
    norm = jnp.sum(square.T, axis=0, keepdims=True)
    info[0] = jnp.broadcast_to(jnp.where(live > 0.5, norm, DEAD), (8, PTS))
    info_to = [(sibling, 1)]
    info_to += [(device_of(q, k, 1 - g), 2 + c) for k in (0, 1)]
    info_to += [(device_of(ahead, k, h), 6 - 2 * c + g) for k in (0, 1) for h in (0, 1)]
    info_to += [(device_of(behind, c, h), 8 + g) for h in (0, 1)]
    info_sends = [
        remote(info.at[0], info.at[s], info_s.at[i], info_r.at[s], to) for i, (to, s) in enumerate(info_to)
    ]
    for send in info_sends:
        send.start()
    loads[2].wait()
    loads[3].wait()
    nb_t[...] = nb_v[...]
    old_t = old_v[...]

    def block_of(s):
        odd = s % 2
        far_pair = jnp.where(s < 8, 4 * up + odd, 4 * ahead + 2 * c + odd)
        far_pair = jnp.where(s < 6, 4 * down + 2 + odd, far_pair)
        near = jnp.where(s == 0, 4 * q + 2 * c + g, 4 * q + 2 * (1 - c) + g)
        near = jnp.where(s < 2, near, 4 * q + 2 * odd + 1 - g)
        return jnp.where(s < 4, near, far_pair)

    def set_bias(s):
        first = block_of(s) * PTS
        ids = first + lax.broadcasted_iota(jnp.int32, (PTS, PTS), 0)
        own_ids = (4 * q + 2 * c + g) * PTS + lax.broadcasted_iota(jnp.int32, (PTS, PTS), 1)
        masked = ids == own_ids
        for k in range(KNN):
            masked = masked | (ids == nb_t[k : k + 1, :])
        key = jnp.broadcast_to(info[s, 0:1, :], (PTS, PTS)).T
        bias[s] = jnp.where(masked, DEAD, key + norm)

    set_bias(0)
    for ref in (gx, gf, gb):
        ref[...] = jnp.zeros_like(ref)
    tiles[0] = jnp.zeros((PTS, PTS), jnp.float32)
    tiles[1] = jnp.zeros((PTS, PTS), jnp.float32)

    def near_blocks(core, j):
        return jnp.concatenate([both[core, :, cols(mine_at, j)], xr[core, :, part(j)]], axis=0)

    def far_products(j):
        for way in (0, 1):
            for h in (0, 1):
                remote(
                    xr.at[way, :, part(j)], fb.at[way, h, :, part(j)], yr_s.at[way, j], f_r.at[way, h, j], sibling
                ).wait_recv()
        v0 = near_blocks(0, j)
        f = fb[1, :, :, part(j)].reshape(2 * PTS, WIDTH)
        gf[0] += dot_nt(f, v0)
        b = fb[0, :, :, part(j)].reshape(2 * PTS, WIDTH)
        gb[...] += dot_nt(b, v0)
        gf[1] += dot_nt(f, near_blocks(1, j))

    def far_quarter(j):
        sib_copy(j).wait_recv()
        quarter = pl.ds(pl.multiple_of(((mine_at + j) % 4) * QUARTER, 128), QUARTER)
        mine = both[c, :, quarter]
        tiles[0] += dot_nt(mine, mine)
        tiles[1] += dot_nt(both[1 - c, :, quarter], mine)

    gx_copy = remote(gx, gx_r, red_s.at[0], red_r.at[0], sibling)
    gf_copy = remote(gf.at[1 - c], gf_r, red_s.at[1], red_r.at[1], sibling)
    gb_copy = remote(gb, gb_r, red_s.at[2], red_r.at[2], sibling)

    for j in range(CHUNKS):

        @pl.when(passes)
        def _(j=j):
            to_middle(0, j).wait_recv()
            pass_on(j).start()

        for way in (0, 1):
            remote(
                pts.at[:, cols(0, 0)], xr.at[way, :, part(j)], x_s.at[0, j], x_r.at[way, j], sibling
            ).wait_recv()
            relay(way, j).start()
        far_quarter(j)
        xs = jnp.concatenate([xr[0, :, part(j)], xr[1, :, part(j)]], axis=0)
        own = jnp.concatenate([both[0, :, cols(mine_at, j)], both[1, :, cols(mine_at, j)]], axis=0)
        gx[...] += dot_nt(xs, own)
        if j == CHUNKS - 1:
            gx_copy.start()
        if j > 0:
            far_products(j - 1)

    gx_copy.wait_recv()
    total = gx[...] + gx_r[...]
    for k in (0, 1):
        hx[k] = total[k * PTS : (k + 1) * PTS]
    other = device_of(q, c, 1 - g)
    rx_copy = remote(hx.at[c], rx, t_s.at[0], rx_sem, other)
    rx_copy.start()

    def each(s, carry):
        remote(info.at[0], info.at[s], info_s.at[0], info_r.at[s], sibling).wait_recv()
        set_bias(s)
        return carry

    lax.fori_loop(1, 10, each, 0)
    far_products(CHUNKS - 1)
    gf_copy.start()

    @pl.when(c == 1)
    def _():
        gb_copy.start()

    gf_copy.wait_recv()
    total = gf[c] + gf_r[...]
    for rel in (0, 1):
        hf[rel] = total[:, rel * PTS : (rel + 1) * PTS]
    rv_copy = remote(hf.at[1], rv, t_s.at[1], rv_sem, other)
    rv_copy.start()

    def ru_copy(src, half_slot, rel, h, sem, to):
        name = g if rel == 0 else 1 - g
        return remote(
            src.at[rel, pl.ds(h * PTS, PTS)], ru.at[g, half_slot, name], sem, ru_sem.at[g, half_slot, name], to
        )

    fu_copies = [
        ru_copy(hf, c, rel, h, t_s.at[2 + 2 * rel + h], device_of(down, 1, h)) for rel in (0, 1) for h in (0, 1)
    ]
    for copy in fu_copies:
        copy.start()
    rbv_copy = remote(hb.at[1], rbv, t_s.at[6], rbv_sem, device_of(q, 0, 1 - g))
    bu_copies = [
        ru_copy(hb, 1, rel, h, t_s.at[7 + 2 * rel + h], device_of(up, 0, h)) for rel in (0, 1) for h in (0, 1)
    ]

    @pl.when(c == 0)
    def _():
        gb_copy.wait_recv()
        for rel in (0, 1):
            half = pl.ds(rel * PTS, PTS)
            hb[rel] = gb[:, half] + gb_r[:, half]
        rbv_copy.start()
        for copy in bu_copies:
            copy.start()

    def taken(best, s, inner):
        value = bias[s]
        dist = jnp.where(value >= 1e34, FAR, (value - 2.0 * inner) / D)
        return merge_lists(best, sort_lists([dist[8 * i : 8 * i + 8] for i in range(KNN)]))

    low, high = jnp.minimum(old_t[:8], old_t[8:]), jnp.maximum(old_t[:8], old_t[8:])
    best = [low, high] + [jnp.full((8, PTS), FAR, jnp.float32)] * (KNN - 2)
    best = taken(best, 0, tiles[0])
    best = taken(best, 1, tiles[1])
    rx_copy.wait_recv()
    lanes = pl.ds(pl.multiple_of(c * PTS, PTS), PTS)
    for k in (0, 1):
        best = taken(best, 2 + k, hx[k, :, lanes] + rx[:, k * PTS : (k + 1) * PTS].T)
    rv_copy.wait_recv()
    for h in (0, 1):
        best = taken(best, 4 + h, hf[0, h * PTS : (h + 1) * PTS] + rv[h * PTS : (h + 1) * PTS])

    def wait_ru(half_slot):
        for half in (0, 1):
            for name in (0, 1):
                remote(
                    hf.at[0, pl.ds(0, PTS)], ru.at[half, half_slot, name], t_s.at[2], ru_sem.at[half, half_slot, name],
                    sibling,
                ).wait_recv()

    @pl.when(c == 0)
    def _():
        rbv_copy.wait_recv()
        for h in (0, 1):
            tiles[2 + h] = hb[0, h * PTS : (h + 1) * PTS] + rbv[h * PTS : (h + 1) * PTS]

    @pl.when(c == 1)
    def _():
        wait_ru(0)
        for h in (0, 1):
            tiles[2 + h] = (ru[0, 0, h] + ru[1, 0, h]).T

    for h in (0, 1):
        best = taken(best, 6 + h, tiles[2 + h])
    wait_ru(1)
    for h in (0, 1):
        best = taken(best, 8 + h, (ru[0, 1, h] + ru[1, 1, h]).T)
    for shift in (4, 2, 1):
        best = merge_lists(best, [pltpu.roll(v, shift, 0) for v in best])

    running = best[KNN - 1][0:1, :]
    sum_copies = []
    first = 0
    for phase, row_peers in enumerate(sum_peers):
        sum_src[phase] = running
        copies = [
            remote(sum_src.at[phase], sum_in.at[first + i], sum_s.at[first + i], sum_r.at[first + i], peer)
            for i, peer in enumerate(row_peers)
        ]
        for copy in copies:
            copy.start()
        for copy in copies:
            copy.wait_recv()
        for i in range(len(copies)):
            running = running + sum_in[first + i]
        sum_copies += copies
        first += len(copies)
    mean = jnp.sum(running, axis=1, keepdims=True) / (PTS * NODES * 4)
    for k in range(KNN):
        out[k : k + 1, :] = best[k][0:1, :] / mean

    for j in range(CHUNKS):
        for k in (0, 1):
            x_copy(k, j).wait_send()
            yo_copy(k, j).wait_send()
            relay(k, j).wait_send()
        sib_copy(j).wait_send()

        @pl.when(passes)
        def _(j=j):
            pass_on(j).wait_send()

    for send in info_sends:
        send.wait_send()
    for copy in [gx_copy, gf_copy, rx_copy, rv_copy, *fu_copies, *sum_copies]:
        copy.wait_send()

    @pl.when(c == 1)
    def _():
        gb_copy.wait_send()

    @pl.when(c == 0)
    def _():
        rbv_copy.wait_send()
        for copy in bu_copies:
            copy.wait_send()


def body(points, cand_index, cand_count, neighbor_ids, old_dist):
    f32, dma = jnp.float32, pltpu.SemaphoreType.DMA
    n_sum = 1 + 15 + 7
    vmem = pltpu.VMEM
    any_spec = pl.BlockSpec(memory_space=pltpu.HBM)
    scratch = [
        vmem((2, PTS, D), f32),
        vmem((2, PTS, QUARTER), f32),
        vmem((2, 2, PTS, QUARTER), f32),
        vmem((256, 256), f32),
        vmem((2, 256, 256), f32),
        vmem((256, 256), f32),
        vmem((256, 256), f32),
        vmem((256, 256), f32),
        vmem((256, 256), f32),
        vmem((2, 128, 256), f32),
        vmem((2, 256, 128), f32),
        vmem((2, 256, 128), f32),
        vmem((128, 256), f32),
        vmem((256, 128), f32),
        vmem((256, 128), f32),
        vmem((2, 2, 2, 128, 128), f32),
        vmem((10, 8, 128), f32),
        vmem((10, 128, 128), f32),
        vmem((4, 128, 128), f32),
        vmem((16, 128), jnp.int32),
        vmem((16, 128), f32),
        vmem((1, 128), jnp.int32),
        vmem((16, 128), jnp.int32),
        vmem((3, 1, 128), f32),
        vmem((n_sum, 1, 128), f32),
        dma((5,)),
        pltpu.SMEM((1,), jnp.int32),
        dma((CHUNKS,)),
        dma((CHUNKS,)),
        dma((2, CHUNKS)),
        dma((2, CHUNKS)),
        dma((2, CHUNKS)),
        dma((2, CHUNKS)),
        dma((2, 2, CHUNKS)),
        dma((9,)),
        dma((10,)),
        dma((3,)),
        dma((3,)),
        vmem((PTS, QUARTER), f32),
        dma((CHUNKS,)),
        dma((CHUNKS,)),
        dma((11,)),
        dma,
        dma,
        dma,
        dma((2, 2, 2)),
        dma((n_sum,)),
        dma((n_sum,)),
    ]
    best = pl.pallas_call(
        kernel,
        out_shape=jax.ShapeDtypeStruct((KNN, PTS), f32),
        in_specs=[any_spec] * 5,
        out_specs=pl.BlockSpec(memory_space=pltpu.VMEM),
        scratch_shapes=scratch,
        compiler_params=pltpu.CompilerParams(
            collective_id=0, has_side_effects=True, vmem_limit_bytes=40 << 20
        ),
    )(points, cand_index, cand_count, neighbor_ids.T, old_dist.T)
    return best.T


def solution(mesh):
    finer = Mesh(mesh.devices.reshape(*SIZES), AXES)
    return jax.shard_map(
        body,
        mesh=finer,
        in_specs=(P(AXES, None), P(AXES, None), P(AXES), P(AXES, None), P(AXES, None)),
        out_specs=P(AXES, None),
        check_vma=False,
    )
```

```python
import functools

import jax
import jax.numpy as jnp
from jax import lax
from jax.experimental import pallas as pl
from jax.experimental.pallas import tpu as pltpu
from jax.sharding import Mesh
from jax.sharding import PartitionSpec as P

AXES = ("xl", "z", "y", "core", "grp")
SIZES = (2, 8, 4, 2, 2)
NODES = 64
MESH = pl.DeviceIdType.MESH
HIGHEST = lax.Precision.HIGHEST
PTS = 128
D = 4096
KNN = 16
QUARTER = 1024
WIDTHS = (256, 256, 256, 256)
CHUNKS = len(WIDTHS)
AHEAD = 3
STARTS = tuple(sum(WIDTHS[:j]) for j in range(CHUNKS))
FAR = 1e30
DEAD = 1e35
SUM_PHASES = ((3,), (0, 4, 2), (1,))


def sort_pairs(n):
    pairs = []
    p = 1
    while p < n:
        k = p
        while k >= 1:
            for j in range(k % p, n - k, 2 * k):
                for i in range(min(k, n - j - k)):
                    if (i + j) // (2 * p) == (i + j + k) // (2 * p):
                        pairs.append((i + j, i + j + k))
            k //= 2
        p *= 2
    return pairs


SORT16 = sort_pairs(KNN)


def sort_lists(values):
    values = list(values)
    for i, j in SORT16:
        low, high = jnp.minimum(values[i], values[j]), jnp.maximum(values[i], values[j])
        values[i], values[j] = low, high
    return values


def merge_lists(a, b):
    m = [jnp.minimum(a[i], b[KNN - 1 - i]) for i in range(KNN)]
    step = KNN // 2
    while step:
        for i in range(KNN):
            if not i & step:
                low, high = jnp.minimum(m[i], m[i + step]), jnp.maximum(m[i], m[i + step])
                m[i], m[i + step] = low, high
        step //= 2
    return m


def dot_nt(a, b):
    return lax.dot_general(
        a, b, (((1,), (1,)), ((), ())), precision=HIGHEST, preferred_element_type=jnp.float32
    )


def device_of(node, core, grp):
    return (node // 32, (node // 4) % 8, node % 4, core, grp)


def kernel(
    pts, cidx, ccnt, nbr, old, out,
    both, xr, fb, gx, gf, gb, gx_r, gf_r, gb_r, hx, hf, hb, rx, rv, rbv, ru,
    info, bias, tiles, nb_v, old_v, ci_v, nb_t, sum_src, sum_in,
    loc_sem, cc_v, sib_s, sib_r, x_s, x_r, yo_s, yr_s, f_r, info_s, info_r, red_s, red_r,
    via, via_s, via_r, t_s, rx_sem, rv_sem, rbv_sem, ru_sem, sum_s, sum_r,
):
    d = tuple(lax.axis_index(a) for a in AXES)
    c, g = d[3], d[4]
    q = d[0] * 32 + d[1] * 4 + d[2]
    up, down = (q + 1) % NODES, (q + NODES - 1) % NODES
    ahead = (q + NODES + 2 * c - 1) % NODES
    behind = (q + NODES + 1 - 2 * c) % NODES
    sibling = device_of(q, 1 - c, g)
    turned = d[0]

    def turn(bit, by):
        return bit + by - 2 * bit * by

    def quarter_at(core, grp):
        return 2 * turn(grp, core * turned) + core

    def same_quarter(node, core, grp):
        return device_of(node, core, turn(grp, core * turn(turned, node // 32)))

    mine_at = quarter_at(c, g)

    def remote(src, dst, send, recv, to):
        return pltpu.make_async_remote_copy(
            src_ref=src, dst_ref=dst, send_sem=send, recv_sem=recv, device_id=to, device_id_type=MESH
        )

    barrier = pltpu.get_barrier_semaphore()
    peers = [device_of(n, k, h) for n in (up, down) for k in (0, 1) for h in (0, 1)]
    peers.append(device_of(q, 1 - c, 1 - g))
    sum_peers = []
    for axes in SUM_PHASES:
        count = 1
        for a in axes:
            count *= SIZES[a]
        row = []
        for offset in range(1, count):
            at, rest = list(d), offset
            for a in axes:
                at[a] = (d[a] + rest % SIZES[a]) % SIZES[a]
                rest //= SIZES[a]
            row.append(tuple(at))
        sum_peers.append(row)
        peers += row
    ring = q % 32
    steps = ((c == 1) & (ring == 31)) | ((c == 0) & (ring == 0))
    passes = (ring == 0) | (ring == 31)
    onward = 1 - ring // 31
    middle = q + 31 - 62 * c
    source = device_of(q - 31 + 62 * onward, onward, g)
    after_node = (1 - d[0]) * 32 + 31 * (1 - onward)
    onward_to = same_quarter(after_node, c, g)

    def greet(peer):
        pl.semaphore_signal(barrier, inc=1, device_id=peer, device_id_type=MESH)

    for peer in peers:
        greet(peer)

    @pl.when(steps)
    def _():
        for k in (0, 1):
            greet(device_of(middle, k, g))

    @pl.when(passes)
    def _():
        greet(source)
        greet(onward_to)

    greeted = len(peers) + jnp.where(steps, 2, 0) + jnp.where(passes, 2, 0)
    loads = [
        pltpu.make_async_copy(pts, both.at[c], loc_sem.at[0]),
        pltpu.make_async_copy(cidx, ci_v, loc_sem.at[1]),
        pltpu.make_async_copy(nbr, nb_v, loc_sem.at[2]),
        pltpu.make_async_copy(old, old_v, loc_sem.at[3]),
        pltpu.make_async_copy(ccnt, cc_v, loc_sem.at[4]),
    ]
    for load in loads:
        load.start()
    pl.semaphore_wait(barrier, greeted)

    def cols(quarter, j):
        return pl.ds(pl.multiple_of(quarter * QUARTER + STARTS[j], 128), WIDTHS[j])

    def part(j):
        return pl.ds(STARTS[j], WIDTHS[j])

    def x_copy(k, j):
        return remote(
            pts.at[:, cols(quarter_at(k, 1 - g), j)], xr.at[c, :, part(j)], x_s.at[k, j], x_r.at[c, j],
            device_of(q, k, 1 - g),
        )

    def yo_copy(k, j):
        return remote(
            pts.at[:, cols(quarter_at(k, g), j)], fb.at[c, g, :, part(j)], yo_s.at[k, j], f_r.at[c, g, j],
            same_quarter(ahead, k, g),
        )

    def to_middle(k, j):
        return remote(
            pts.at[:, cols(quarter_at(k, g), j)], via.at[:, part(j)], yo_s.at[k, j], via_r.at[j],
            device_of(middle, k, g),
        )

    def pass_on(j):
        return remote(
            via.at[:, part(j)], fb.at[onward, g, :, part(j)], via_s.at[j], f_r.at[onward, g, j], onward_to
        )

    def sib_copy(i):
        quarter = pl.ds(pl.multiple_of(((quarter_at(1 - c, g) + i) % 4) * QUARTER, 128), QUARTER)
        return remote(pts.at[:, quarter], both.at[c, :, quarter], sib_s.at[i], sib_r.at[i], sibling)

    def relay(way, j):
        to = same_quarter(up if way else down, c, g)
        return remote(
            xr.at[way, :, part(j)], fb.at[way, 1 - g, :, part(j)], yr_s.at[way, j], f_r.at[way, 1 - g, j], to
        )

    for j in range(CHUNKS):
        for k in (0, 1):
            if j < AHEAD:
                x_copy(k, j).start()

            @pl.when(steps)
            def _(k=k, j=j):
                to_middle(k, j).start()

            @pl.when(jnp.logical_not(steps))
            def _(k=k, j=j):
                yo_copy(k, j).start()

    for i in range(4):
        sib_copy(i).start()

    loads[1].wait()
    loads[4].wait()
    slot = lax.broadcasted_iota(jnp.int32, (PTS, PTS), 1)
    row = lax.broadcasted_iota(jnp.int32, (PTS, PTS), 0)
    hit = (jnp.broadcast_to(ci_v[...], (PTS, PTS)) == row) & (slot < cc_v[0])
    live = jnp.max(jnp.where(hit, 1.0, 0.0).T, axis=0, keepdims=True)
    loads[0].wait()
    square = jnp.zeros((PTS, PTS), jnp.float32)
    for i in range(D // PTS):
        x = both[c, :, i * PTS : (i + 1) * PTS]
        square = square + x * x
    norm = jnp.sum(square.T, axis=0, keepdims=True)
    info[0] = jnp.broadcast_to(jnp.where(live > 0.5, norm, DEAD), (8, PTS))
    info_to = [(sibling, 1)]
    info_to += [(device_of(q, k, 1 - g), 2 + c) for k in (0, 1)]
    info_to += [(device_of(ahead, k, h), 6 - 2 * c + g) for k in (0, 1) for h in (0, 1)]
    info_to += [(device_of(behind, c, h), 8 + g) for h in (0, 1)]
    info_sends = [
        remote(info.at[0], info.at[s], info_s.at[i], info_r.at[s], to) for i, (to, s) in enumerate(info_to)
    ]
    for send in info_sends:
        send.start()
    loads[2].wait()
    loads[3].wait()
    nb_t[...] = nb_v[...]
    old_t = old_v[...]

    def block_of(s):
        odd = s % 2
        far_pair = jnp.where(s < 8, 4 * up + odd, 4 * ahead + 2 * c + odd)
        far_pair = jnp.where(s < 6, 4 * down + 2 + odd, far_pair)
        near = jnp.where(s == 0, 4 * q + 2 * c + g, 4 * q + 2 * (1 - c) + g)
        near = jnp.where(s < 2, near, 4 * q + 2 * odd + 1 - g)
        return jnp.where(s < 4, near, far_pair)

    def set_bias(s):
        first = block_of(s) * PTS
        ids = first + lax.broadcasted_iota(jnp.int32, (PTS, PTS), 0)
        own_ids = (4 * q + 2 * c + g) * PTS + lax.broadcasted_iota(jnp.int32, (PTS, PTS), 1)
        masked = ids == own_ids
        for k in range(KNN):
            masked = masked | (ids == nb_t[k : k + 1, :])
        key = jnp.broadcast_to(info[s, 0:1, :], (PTS, PTS)).T
        bias[s] = jnp.where(masked, DEAD, key + norm)

    set_bias(0)
    for ref in (gx, gf, gb):
        ref[...] = jnp.zeros_like(ref)
    tiles[0] = jnp.zeros((PTS, PTS), jnp.float32)
    tiles[1] = jnp.zeros((PTS, PTS), jnp.float32)

    def near_blocks(core, j):
        return jnp.concatenate([both[core, :, cols(mine_at, j)], xr[core, :, part(j)]], axis=0)

    def far_products(j):
        for way in (0, 1):
            for h in (0, 1):
                remote(
                    xr.at[way, :, part(j)], fb.at[way, h, :, part(j)], yr_s.at[way, j], f_r.at[way, h, j], sibling
                ).wait_recv()
        f = fb[1, :, :, part(j)].reshape(2 * PTS, WIDTHS[j])
        gf[1 - c] += dot_nt(f, near_blocks(1 - c, j))
        if j == CHUNKS - 1:
            gf_copy.start()
        b = fb[0, :, :, part(j)].reshape(2 * PTS, WIDTHS[j])
        gb[...] += dot_nt(b, near_blocks(0, j))
        if j == CHUNKS - 1:
            pl.when(c == 1)(gb_copy.start)
        gf[c] += dot_nt(f, near_blocks(c, j))

    def far_quarter(j):
        sib_copy(j).wait_recv()
        quarter = pl.ds(pl.multiple_of(((mine_at + j) % 4) * QUARTER, 128), QUARTER)
        mine = both[c, :, quarter]
        tiles[0] += dot_nt(mine, mine)
        tiles[1] += dot_nt(both[1 - c, :, quarter], mine)

    gx_copy = remote(gx, gx_r, red_s.at[0], red_r.at[0], sibling)
    gf_copy = remote(gf.at[1 - c], gf_r, red_s.at[1], red_r.at[1], sibling)
    gb_copy = remote(gb, gb_r, red_s.at[2], red_r.at[2], sibling)

    for j in range(CHUNKS):

        @pl.when(passes)
        def _(j=j):
            to_middle(0, j).wait_recv()
            pass_on(j).start()

        for way in (0, 1):
            remote(
                pts.at[:, cols(0, j)], xr.at[way, :, part(j)], x_s.at[0, j], x_r.at[way, j], sibling
            ).wait_recv()
            relay(way, j).start()
        if j + AHEAD < CHUNKS:
            for k in (0, 1):
                x_copy(k, j + AHEAD).start()
        for i in range(4):
            if i * CHUNKS // 4 == j:
                far_quarter(i)
        xs = jnp.concatenate([xr[0, :, part(j)], xr[1, :, part(j)]], axis=0)
        own = jnp.concatenate([both[0, :, cols(mine_at, j)], both[1, :, cols(mine_at, j)]], axis=0)
        gx[...] += dot_nt(xs, own)
        if j == CHUNKS - 1:
            gx_copy.start()
        if j > 0:
            far_products(j - 1)

    gx_copy.wait_recv()
    total = gx[...] + gx_r[...]
    for k in (0, 1):
        hx[k] = total[k * PTS : (k + 1) * PTS]
    other = device_of(q, c, 1 - g)
    rx_copy = remote(hx.at[c], rx, t_s.at[0], rx_sem, other)
    rx_copy.start()

    def each(s, carry):
        remote(info.at[0], info.at[s], info_s.at[0], info_r.at[s], sibling).wait_recv()
        set_bias(s)
        return carry

    lax.fori_loop(1, 10, each, 0)
    far_products(CHUNKS - 1)
    gf_copy.wait_recv()
    total = gf[c] + gf_r[...]
    for rel in (0, 1):
        hf[rel] = total[:, rel * PTS : (rel + 1) * PTS]
    rv_copy = remote(hf.at[1], rv, t_s.at[1], rv_sem, other)
    rv_copy.start()

    def ru_copy(src, half_slot, rel, h, sem, to):
        name = g if rel == 0 else 1 - g
        return remote(
            src.at[rel, pl.ds(h * PTS, PTS)], ru.at[g, half_slot, name], sem, ru_sem.at[g, half_slot, name], to
        )

    fu_copies = [
        ru_copy(hf, c, rel, h, t_s.at[2 + 2 * rel + h], device_of(down, 1, h)) for rel in (0, 1) for h in (0, 1)
    ]
    for copy in fu_copies:
        copy.start()
    rbv_copy = remote(hb.at[1], rbv, t_s.at[6], rbv_sem, device_of(q, 0, 1 - g))
    bu_copies = [
        ru_copy(hb, 1, rel, h, t_s.at[7 + 2 * rel + h], device_of(up, 0, h)) for rel in (0, 1) for h in (0, 1)
    ]

    @pl.when(c == 0)
    def _():
        gb_copy.wait_recv()
        for rel in (0, 1):
            half = pl.ds(rel * PTS, PTS)
            hb[rel] = gb[:, half] + gb_r[:, half]
        rbv_copy.start()
        for copy in bu_copies:
            copy.start()

    def taken(best, s, inner):
        value = bias[s]
        dist = jnp.where(value >= 1e34, FAR, (value - 2.0 * inner) / D)
        return merge_lists(best, sort_lists([dist[8 * i : 8 * i + 8] for i in range(KNN)]))

    low, high = jnp.minimum(old_t[:8], old_t[8:]), jnp.maximum(old_t[:8], old_t[8:])
    best = [low, high] + [jnp.full((8, PTS), FAR, jnp.float32)] * (KNN - 2)
    best = taken(best, 0, tiles[0])
    best = taken(best, 1, tiles[1])
    rx_copy.wait_recv()
    lanes = pl.ds(pl.multiple_of(c * PTS, PTS), PTS)
    for k in (0, 1):
        best = taken(best, 2 + k, hx[k, :, lanes] + rx[:, k * PTS : (k + 1) * PTS].T)
    rv_copy.wait_recv()
    for h in (0, 1):
        best = taken(best, 4 + h, hf[0, h * PTS : (h + 1) * PTS] + rv[h * PTS : (h + 1) * PTS])

    def wait_ru(half_slot):
        for half in (0, 1):
            for name in (0, 1):
                remote(
                    hf.at[0, pl.ds(0, PTS)], ru.at[half, half_slot, name], t_s.at[2], ru_sem.at[half, half_slot, name],
                    sibling,
                ).wait_recv()

    @pl.when(c == 0)
    def _():
        rbv_copy.wait_recv()
        for h in (0, 1):
            tiles[2 + h] = hb[0, h * PTS : (h + 1) * PTS] + rbv[h * PTS : (h + 1) * PTS]

    @pl.when(c == 1)
    def _():
        wait_ru(0)
        for h in (0, 1):
            tiles[2 + h] = (ru[0, 0, h] + ru[1, 0, h]).T

    for h in (0, 1):
        best = taken(best, 6 + h, tiles[2 + h])
    wait_ru(1)
    for h in (0, 1):
        best = taken(best, 8 + h, (ru[0, 1, h] + ru[1, 1, h]).T)
    for shift in (4, 2, 1):
        best = merge_lists(best, [pltpu.roll(v, shift, 0) for v in best])

    running = best[KNN - 1][0:1, :]
    sum_copies = []
    first = 0
    for phase, row_peers in enumerate(sum_peers):
        sum_src[phase] = running
        copies = [
            remote(sum_src.at[phase], sum_in.at[first + i], sum_s.at[first + i], sum_r.at[first + i], peer)
            for i, peer in enumerate(row_peers)
        ]
        for copy in copies:
            copy.start()
        for copy in copies:
            copy.wait_recv()
        for i in range(len(copies)):
            running = running + sum_in[first + i]
        sum_copies += copies
        first += len(copies)
    mean = jnp.sum(running, axis=1, keepdims=True) / (PTS * NODES * 4)
    for k in range(KNN):
        out[k : k + 1, :] = best[k][0:1, :] / mean

    for j in range(CHUNKS):
        for k in (0, 1):
            x_copy(k, j).wait_send()
            yo_copy(k, j).wait_send()
            relay(k, j).wait_send()

        @pl.when(passes)
        def _(j=j):
            pass_on(j).wait_send()

    for i in range(4):
        sib_copy(i).wait_send()
    for send in info_sends:
        send.wait_send()
    for copy in [gx_copy, gf_copy, rx_copy, rv_copy, *fu_copies, *sum_copies]:
        copy.wait_send()

    @pl.when(c == 1)
    def _():
        gb_copy.wait_send()

    @pl.when(c == 0)
    def _():
        rbv_copy.wait_send()
        for copy in bu_copies:
            copy.wait_send()


def body(points, cand_index, cand_count, neighbor_ids, old_dist):
    f32, dma = jnp.float32, pltpu.SemaphoreType.DMA
    n_sum = 1 + 15 + 7
    vmem = pltpu.VMEM
    any_spec = pl.BlockSpec(memory_space=pltpu.HBM)
    scratch = [
        vmem((2, PTS, D), f32),
        vmem((2, PTS, QUARTER), f32),
        vmem((2, 2, PTS, QUARTER), f32),
        vmem((256, 256), f32),
        vmem((2, 256, 256), f32),
        vmem((256, 256), f32),
        vmem((256, 256), f32),
        vmem((256, 256), f32),
        vmem((256, 256), f32),
        vmem((2, 128, 256), f32),
        vmem((2, 256, 128), f32),
        vmem((2, 256, 128), f32),
        vmem((128, 256), f32),
        vmem((256, 128), f32),
        vmem((256, 128), f32),
        vmem((2, 2, 2, 128, 128), f32),
        vmem((10, 8, 128), f32),
        vmem((10, 128, 128), f32),
        vmem((4, 128, 128), f32),
        vmem((16, 128), jnp.int32),
        vmem((16, 128), f32),
        vmem((1, 128), jnp.int32),
        vmem((16, 128), jnp.int32),
        vmem((3, 1, 128), f32),
        vmem((n_sum, 1, 128), f32),
        dma((5,)),
        pltpu.SMEM((1,), jnp.int32),
        dma((CHUNKS,)),
        dma((CHUNKS,)),
        dma((2, CHUNKS)),
        dma((2, CHUNKS)),
        dma((2, CHUNKS)),
        dma((2, CHUNKS)),
        dma((2, 2, CHUNKS)),
        dma((9,)),
        dma((10,)),
        dma((3,)),
        dma((3,)),
        vmem((PTS, QUARTER), f32),
        dma((CHUNKS,)),
        dma((CHUNKS,)),
        dma((11,)),
        dma,
        dma,
        dma,
        dma((2, 2, 2)),
        dma((n_sum,)),
        dma((n_sum,)),
    ]
    best = pl.pallas_call(
        kernel,
        out_shape=jax.ShapeDtypeStruct((KNN, PTS), f32),
        in_specs=[any_spec] * 5,
        out_specs=pl.BlockSpec(memory_space=pltpu.VMEM),
        scratch_shapes=scratch,
        compiler_params=pltpu.CompilerParams(
            collective_id=0, has_side_effects=True, vmem_limit_bytes=40 << 20
        ),
    )(points, cand_index, cand_count, neighbor_ids.T, old_dist.T)
    return best.T


def solution(mesh):
    finer = Mesh(mesh.devices.reshape(*SIZES), AXES)
    return jax.shard_map(
        body,
        mesh=finer,
        in_specs=(P(AXES, None), P(AXES, None), P(AXES), P(AXES, None), P(AXES, None)),
        out_specs=P(AXES, None),
        check_vma=False,
    )
```

```python
import functools

import jax
import jax.numpy as jnp
from jax import lax
from jax.experimental import pallas as pl
from jax.experimental.pallas import tpu as pltpu
from jax.sharding import Mesh
from jax.sharding import PartitionSpec as P

AXES = ("xl", "z", "y", "core", "grp")
SIZES = (2, 8, 4, 2, 2)
NODES = 64
MESH = pl.DeviceIdType.MESH
HIGHEST = lax.Precision.HIGHEST
PTS = 128
D = 4096
KNN = 16
QUARTER = 1024
WIDTHS = (256, 256, 256, 256)
CHUNKS = len(WIDTHS)
AHEAD = 3
STARTS = tuple(sum(WIDTHS[:j]) for j in range(CHUNKS))
FAR = 1e30
DEAD = 1e35
SUM_PHASES = ((3,), (0, 4, 2), (1,))


def sort_pairs(n):
    pairs = []
    p = 1
    while p < n:
        k = p
        while k >= 1:
            for j in range(k % p, n - k, 2 * k):
                for i in range(min(k, n - j - k)):
                    if (i + j) // (2 * p) == (i + j + k) // (2 * p):
                        pairs.append((i + j, i + j + k))
            k //= 2
        p *= 2
    return pairs


SORT16 = sort_pairs(KNN)


def sort_lists(values):
    values = list(values)
    for i, j in SORT16:
        low, high = jnp.minimum(values[i], values[j]), jnp.maximum(values[i], values[j])
        values[i], values[j] = low, high
    return values


def merge_lists(a, b):
    m = [jnp.minimum(a[i], b[KNN - 1 - i]) for i in range(KNN)]
    step = KNN // 2
    while step:
        for i in range(KNN):
            if not i & step:
                low, high = jnp.minimum(m[i], m[i + step]), jnp.maximum(m[i], m[i + step])
                m[i], m[i + step] = low, high
        step //= 2
    return m


def dot_nt(a, b):
    return lax.dot_general(
        a, b, (((1,), (1,)), ((), ())), precision=HIGHEST, preferred_element_type=jnp.float32
    )


def device_of(node, core, grp):
    return (node // 32, (node // 4) % 8, node % 4, core, grp)


def kernel(
    pts, cidx, ccnt, nbr, old, out,
    both, xr, fb, gx, gf, gb, gx_r, gf_r, gb_r, hx, hf, hb, rx, rv, rbv, ru,
    info, bias, tiles, nb_v, old_v, ci_v, nb_t, sum_src, sum_in,
    loc_sem, cc_v, sib_s, sib_r, x_s, x_r, yo_s, yr_s, f_r, info_s, info_r, red_s, red_r,
    via, via_s, via_r, t_s, rx_sem, rv_sem, rbv_sem, ru_sem, sum_s, sum_r,
):
    d = tuple(lax.axis_index(a) for a in AXES)
    c, g = d[3], d[4]
    q = d[0] * 32 + d[1] * 4 + d[2]
    up, down = (q + 1) % NODES, (q + NODES - 1) % NODES
    ahead = (q + NODES + 2 * c - 1) % NODES
    behind = (q + NODES + 1 - 2 * c) % NODES
    sibling = device_of(q, 1 - c, g)
    turned = d[0]

    def turn(bit, by):
        return bit + by - 2 * bit * by

    def quarter_at(core, grp):
        return 2 * turn(grp, core * turned) + core

    def same_quarter(node, core, grp):
        return device_of(node, core, turn(grp, core * turn(turned, node // 32)))

    mine_at = quarter_at(c, g)

    def remote(src, dst, send, recv, to):
        return pltpu.make_async_remote_copy(
            src_ref=src, dst_ref=dst, send_sem=send, recv_sem=recv, device_id=to, device_id_type=MESH
        )

    barrier = pltpu.get_barrier_semaphore()
    peers = [device_of(n, k, h) for n in (up, down) for k in (0, 1) for h in (0, 1)]
    peers.append(device_of(q, 1 - c, 1 - g))
    sum_peers = []
    for axes in SUM_PHASES:
        count = 1
        for a in axes:
            count *= SIZES[a]
        row = []
        for offset in range(1, count):
            at, rest = list(d), offset
            for a in axes:
                at[a] = (d[a] + rest % SIZES[a]) % SIZES[a]
                rest //= SIZES[a]
            row.append(tuple(at))
        sum_peers.append(row)
        peers += row
    ring = q % 32
    steps = ((c == 1) & (ring == 31)) | ((c == 0) & (ring == 0))
    passes = (ring == 0) | (ring == 31)
    onward = 1 - ring // 31
    middle = q + 31 - 62 * c
    source = device_of(q - 31 + 62 * onward, onward, g)
    after_node = (1 - d[0]) * 32 + 31 * (1 - onward)
    onward_to = same_quarter(after_node, c, g)

    def greet(peer):
        pl.semaphore_signal(barrier, inc=1, device_id=peer, device_id_type=MESH)

    for peer in peers:
        greet(peer)

    @pl.when(steps)
    def _():
        for k in (0, 1):
            greet(device_of(middle, k, g))

    @pl.when(passes)
    def _():
        greet(source)
        greet(onward_to)

    greeted = len(peers) + jnp.where(steps, 2, 0) + jnp.where(passes, 2, 0)
    loads = [
        pltpu.make_async_copy(pts, both.at[c], loc_sem.at[0]),
        pltpu.make_async_copy(cidx, ci_v, loc_sem.at[1]),
        pltpu.make_async_copy(nbr, nb_v, loc_sem.at[2]),
        pltpu.make_async_copy(old, old_v, loc_sem.at[3]),
        pltpu.make_async_copy(ccnt, cc_v, loc_sem.at[4]),
    ]
    for load in loads:
        load.start()
    pl.semaphore_wait(barrier, greeted)

    def cols(quarter, j):
        return pl.ds(pl.multiple_of(quarter * QUARTER + STARTS[j], 128), WIDTHS[j])

    def part(j):
        return pl.ds(STARTS[j], WIDTHS[j])

    def x_copy(k, j):
        return remote(
            pts.at[:, cols(quarter_at(k, 1 - g), j)], xr.at[c, :, part(j)], x_s.at[k, j], x_r.at[c, j],
            device_of(q, k, 1 - g),
        )

    def yo_copy(k, j):
        return remote(
            pts.at[:, cols(quarter_at(k, g), j)], fb.at[c, g, :, part(j)], yo_s.at[k, j], f_r.at[c, g, j],
            same_quarter(ahead, k, g),
        )

    def to_middle(k, j):
        return remote(
            pts.at[:, cols(quarter_at(k, g), j)], via.at[:, part(j)], yo_s.at[k, j], via_r.at[j],
            device_of(middle, k, g),
        )

    def pass_on(j):
        return remote(
            via.at[:, part(j)], fb.at[onward, g, :, part(j)], via_s.at[j], f_r.at[onward, g, j], onward_to
        )

    def sib_copy(i):
        quarter = pl.ds(pl.multiple_of(((quarter_at(1 - c, g) + i) % 4) * QUARTER, 128), QUARTER)
        return remote(pts.at[:, quarter], both.at[c, :, quarter], sib_s.at[i], sib_r.at[i], sibling)

    def relay(way, j):
        to = same_quarter(up if way else down, c, g)
        return remote(
            xr.at[way, :, part(j)], fb.at[way, 1 - g, :, part(j)], yr_s.at[way, j], f_r.at[way, 1 - g, j], to
        )

    def yo_start(k, j):
        @pl.when(steps)
        def _():
            to_middle(k, j).start()

        @pl.when(jnp.logical_not(steps))
        def _():
            yo_copy(k, j).start()

    for j in range(CHUNKS):
        for k in (0, 1):
            if j < AHEAD:
                x_copy(k, j).start()
                yo_start(k, j)
    for i in range(4):
        sib_copy(i).start()

    loads[1].wait()
    loads[4].wait()
    slot = lax.broadcasted_iota(jnp.int32, (PTS, PTS), 1)
    row = lax.broadcasted_iota(jnp.int32, (PTS, PTS), 0)
    hit = (jnp.broadcast_to(ci_v[...], (PTS, PTS)) == row) & (slot < cc_v[0])
    live = jnp.max(jnp.where(hit, 1.0, 0.0).T, axis=0, keepdims=True)
    loads[0].wait()
    square = jnp.zeros((PTS, PTS), jnp.float32)
    for i in range(D // PTS):
        x = both[c, :, i * PTS : (i + 1) * PTS]
        square = square + x * x
    norm = jnp.sum(square.T, axis=0, keepdims=True)
    info[0] = jnp.broadcast_to(jnp.where(live > 0.5, norm, DEAD), (8, PTS))
    info_to = [(sibling, 1)]
    info_to += [(device_of(q, k, 1 - g), 2 + c) for k in (0, 1)]
    info_to += [(device_of(ahead, k, h), 6 - 2 * c + g) for k in (0, 1) for h in (0, 1)]
    info_to += [(device_of(behind, c, h), 8 + g) for h in (0, 1)]
    info_sends = [
        remote(info.at[0], info.at[s], info_s.at[i], info_r.at[s], to) for i, (to, s) in enumerate(info_to)
    ]
    for send in info_sends:
        send.start()
    loads[2].wait()
    loads[3].wait()
    nb_t[...] = nb_v[...]
    old_t = old_v[...]

    def block_of(s):
        odd = s % 2
        far_pair = jnp.where(s < 8, 4 * up + odd, 4 * ahead + 2 * c + odd)
        far_pair = jnp.where(s < 6, 4 * down + 2 + odd, far_pair)
        near = jnp.where(s == 0, 4 * q + 2 * c + g, 4 * q + 2 * (1 - c) + g)
        near = jnp.where(s < 2, near, 4 * q + 2 * odd + 1 - g)
        return jnp.where(s < 4, near, far_pair)

    def set_bias(s):
        first = block_of(s) * PTS
        ids = first + lax.broadcasted_iota(jnp.int32, (PTS, PTS), 0)
        own_ids = (4 * q + 2 * c + g) * PTS + lax.broadcasted_iota(jnp.int32, (PTS, PTS), 1)
        masked = ids == own_ids
        for k in range(KNN):
            masked = masked | (ids == nb_t[k : k + 1, :])
        key = jnp.broadcast_to(info[s, 0:1, :], (PTS, PTS)).T
        bias[s] = jnp.where(masked, DEAD, key + norm)

    set_bias(0)
    for ref in (gx, gf, gb):
        ref[...] = jnp.zeros_like(ref)
    tiles[0] = jnp.zeros((PTS, PTS), jnp.float32)
    tiles[1] = jnp.zeros((PTS, PTS), jnp.float32)

    def near_blocks(core, j):
        return jnp.concatenate([both[core, :, cols(mine_at, j)], xr[core, :, part(j)]], axis=0)

    def far_products(j):
        for way in (0, 1):
            for h in (0, 1):
                remote(
                    xr.at[way, :, part(j)], fb.at[way, h, :, part(j)], yr_s.at[way, j], f_r.at[way, h, j], sibling
                ).wait_recv()
        f = fb[1, :, :, part(j)].reshape(2 * PTS, WIDTHS[j])
        gf[1 - c] += dot_nt(f, near_blocks(1 - c, j))
        if j == CHUNKS - 1:
            gf_copy.start()
        b = fb[0, :, :, part(j)].reshape(2 * PTS, WIDTHS[j])
        gb[...] += dot_nt(b, near_blocks(0, j))
        if j == CHUNKS - 1:
            pl.when(c == 1)(gb_copy.start)
        gf[c] += dot_nt(f, near_blocks(c, j))

    def far_quarter(j):
        sib_copy(j).wait_recv()
        quarter = pl.ds(pl.multiple_of(((mine_at + j) % 4) * QUARTER, 128), QUARTER)
        mine = both[c, :, quarter]
        tiles[0] += dot_nt(mine, mine)
        tiles[1] += dot_nt(both[1 - c, :, quarter], mine)

    gx_copy = remote(gx, gx_r, red_s.at[0], red_r.at[0], sibling)
    gf_copy = remote(gf.at[1 - c], gf_r, red_s.at[1], red_r.at[1], sibling)
    gb_copy = remote(gb, gb_r, red_s.at[2], red_r.at[2], sibling)

    for j in range(CHUNKS):

        @pl.when(passes)
        def _(j=j):
            to_middle(0, j).wait_recv()
            pass_on(j).start()

        for way in (0, 1):
            remote(
                pts.at[:, cols(0, j)], xr.at[way, :, part(j)], x_s.at[0, j], x_r.at[way, j], sibling
            ).wait_recv()
            relay(way, j).start()
        if j + AHEAD < CHUNKS:
            for k in (0, 1):
                x_copy(k, j + AHEAD).start()
                yo_start(k, j + AHEAD)
        for i in range(4):
            if max(i - 1, 0) == j:
                far_quarter(i)
        xs = jnp.concatenate([xr[0, :, part(j)], xr[1, :, part(j)]], axis=0)
        own = jnp.concatenate([both[0, :, cols(mine_at, j)], both[1, :, cols(mine_at, j)]], axis=0)
        gx[...] += dot_nt(xs, own)
        if j == CHUNKS - 2:
            def each(s, carry):
                remote(info.at[0], info.at[s], info_s.at[0], info_r.at[s], sibling).wait_recv()
                set_bias(s)
                return carry

            lax.fori_loop(1, 10, each, 0)
        if j == CHUNKS - 1:
            gx_copy.start()
        if j > 0:
            far_products(j - 1)

    gx_copy.wait_recv()
    total = gx[...] + gx_r[...]
    for k in (0, 1):
        hx[k] = total[k * PTS : (k + 1) * PTS]
    other = device_of(q, c, 1 - g)
    rx_copy = remote(hx.at[c], rx, t_s.at[0], rx_sem, other)
    rx_copy.start()

    far_products(CHUNKS - 1)
    gf_copy.wait_recv()
    total = gf[c] + gf_r[...]
    for rel in (0, 1):
        hf[rel] = total[:, rel * PTS : (rel + 1) * PTS]
    rv_copy = remote(hf.at[1], rv, t_s.at[1], rv_sem, other)
    rv_copy.start()

    def ru_copy(src, half_slot, rel, h, sem, to):
        name = g if rel == 0 else 1 - g
        return remote(
            src.at[rel, pl.ds(h * PTS, PTS)], ru.at[g, half_slot, name], sem, ru_sem.at[g, half_slot, name], to
        )

    fu_copies = [
        ru_copy(hf, c, rel, h, t_s.at[2 + 2 * rel + h], device_of(down, 1, h)) for rel in (0, 1) for h in (0, 1)
    ]
    for copy in fu_copies:
        copy.start()
    rbv_copy = remote(hb.at[1], rbv, t_s.at[6], rbv_sem, device_of(q, 0, 1 - g))
    bu_copies = [
        ru_copy(hb, 1, rel, h, t_s.at[7 + 2 * rel + h], device_of(up, 0, h)) for rel in (0, 1) for h in (0, 1)
    ]

    @pl.when(c == 0)
    def _():
        gb_copy.wait_recv()
        for rel in (0, 1):
            half = pl.ds(rel * PTS, PTS)
            hb[rel] = gb[:, half] + gb_r[:, half]
        rbv_copy.start()
        for copy in bu_copies:
            copy.start()

    def taken(best, s, inner):
        value = bias[s]
        dist = jnp.where(value >= 1e34, FAR, (value - 2.0 * inner) / D)
        return merge_lists(best, sort_lists([dist[8 * i : 8 * i + 8] for i in range(KNN)]))

    low, high = jnp.minimum(old_t[:8], old_t[8:]), jnp.maximum(old_t[:8], old_t[8:])
    best = [low, high] + [jnp.full((8, PTS), FAR, jnp.float32)] * (KNN - 2)
    best = taken(best, 0, tiles[0])
    best = taken(best, 1, tiles[1])
    rx_copy.wait_recv()
    lanes = pl.ds(pl.multiple_of(c * PTS, PTS), PTS)
    for k in (0, 1):
        best = taken(best, 2 + k, hx[k, :, lanes] + rx[:, k * PTS : (k + 1) * PTS].T)
    rv_copy.wait_recv()
    for h in (0, 1):
        best = taken(best, 4 + h, hf[0, h * PTS : (h + 1) * PTS] + rv[h * PTS : (h + 1) * PTS])

    def wait_ru(half_slot):
        for half in (0, 1):
            for name in (0, 1):
                remote(
                    hf.at[0, pl.ds(0, PTS)], ru.at[half, half_slot, name], t_s.at[2], ru_sem.at[half, half_slot, name],
                    sibling,
                ).wait_recv()

    @pl.when(c == 0)
    def _():
        rbv_copy.wait_recv()
        for h in (0, 1):
            tiles[2 + h] = hb[0, h * PTS : (h + 1) * PTS] + rbv[h * PTS : (h + 1) * PTS]

    @pl.when(c == 1)
    def _():
        wait_ru(0)
        for h in (0, 1):
            tiles[2 + h] = (ru[0, 0, h] + ru[1, 0, h]).T

    for h in (0, 1):
        best = taken(best, 6 + h, tiles[2 + h])
    wait_ru(1)
    for h in (0, 1):
        best = taken(best, 8 + h, (ru[0, 1, h] + ru[1, 1, h]).T)
    for shift in (4, 2, 1):
        best = merge_lists(best, [pltpu.roll(v, shift, 0) for v in best])

    running = best[KNN - 1][0:1, :]
    sum_copies = []
    first = 0
    for phase, row_peers in enumerate(sum_peers):
        sum_src[phase] = running
        copies = [
            remote(sum_src.at[phase], sum_in.at[first + i], sum_s.at[first + i], sum_r.at[first + i], peer)
            for i, peer in enumerate(row_peers)
        ]
        for copy in copies:
            copy.start()
        for copy in copies:
            copy.wait_recv()
        for i in range(len(copies)):
            running = running + sum_in[first + i]
        sum_copies += copies
        first += len(copies)
    mean = jnp.sum(running, axis=1, keepdims=True) / (PTS * NODES * 4)
    for k in range(KNN):
        out[k : k + 1, :] = best[k][0:1, :] / mean

    for j in range(CHUNKS):
        for k in (0, 1):
            x_copy(k, j).wait_send()
            yo_copy(k, j).wait_send()
            relay(k, j).wait_send()

        @pl.when(passes)
        def _(j=j):
            pass_on(j).wait_send()

    for i in range(4):
        sib_copy(i).wait_send()
    for send in info_sends:
        send.wait_send()
    for copy in [gx_copy, gf_copy, rx_copy, rv_copy, *fu_copies, *sum_copies]:
        copy.wait_send()

    @pl.when(c == 1)
    def _():
        gb_copy.wait_send()

    @pl.when(c == 0)
    def _():
        rbv_copy.wait_send()
        for copy in bu_copies:
            copy.wait_send()


def body(points, cand_index, cand_count, neighbor_ids, old_dist):
    f32, dma = jnp.float32, pltpu.SemaphoreType.DMA
    n_sum = 1 + 15 + 7
    vmem = pltpu.VMEM
    any_spec = pl.BlockSpec(memory_space=pltpu.HBM)
    scratch = [
        vmem((2, PTS, D), f32),
        vmem((2, PTS, QUARTER), f32),
        vmem((2, 2, PTS, QUARTER), f32),
        vmem((256, 256), f32),
        vmem((2, 256, 256), f32),
        vmem((256, 256), f32),
        vmem((256, 256), f32),
        vmem((256, 256), f32),
        vmem((256, 256), f32),
        vmem((2, 128, 256), f32),
        vmem((2, 256, 128), f32),
        vmem((2, 256, 128), f32),
        vmem((128, 256), f32),
        vmem((256, 128), f32),
        vmem((256, 128), f32),
        vmem((2, 2, 2, 128, 128), f32),
        vmem((10, 8, 128), f32),
        vmem((10, 128, 128), f32),
        vmem((4, 128, 128), f32),
        vmem((16, 128), jnp.int32),
        vmem((16, 128), f32),
        vmem((1, 128), jnp.int32),
        vmem((16, 128), jnp.int32),
        vmem((3, 1, 128), f32),
        vmem((n_sum, 1, 128), f32),
        dma((5,)),
        pltpu.SMEM((1,), jnp.int32),
        dma((CHUNKS,)),
        dma((CHUNKS,)),
        dma((2, CHUNKS)),
        dma((2, CHUNKS)),
        dma((2, CHUNKS)),
        dma((2, CHUNKS)),
        dma((2, 2, CHUNKS)),
        dma((9,)),
        dma((10,)),
        dma((3,)),
        dma((3,)),
        vmem((PTS, QUARTER), f32),
        dma((CHUNKS,)),
        dma((CHUNKS,)),
        dma((11,)),
        dma,
        dma,
        dma,
        dma((2, 2, 2)),
        dma((n_sum,)),
        dma((n_sum,)),
    ]
    best = pl.pallas_call(
        kernel,
        out_shape=jax.ShapeDtypeStruct((KNN, PTS), f32),
        in_specs=[any_spec] * 5,
        out_specs=pl.BlockSpec(memory_space=pltpu.VMEM),
        scratch_shapes=scratch,
        compiler_params=pltpu.CompilerParams(
            collective_id=0, has_side_effects=True, vmem_limit_bytes=40 << 20
        ),
    )(points, cand_index, cand_count, neighbor_ids.T, old_dist.T)
    return best.T


def solution(mesh):
    finer = Mesh(mesh.devices.reshape(*SIZES), AXES)
    return jax.shard_map(
        body,
        mesh=finer,
        in_specs=(P(AXES, None), P(AXES, None), P(AXES), P(AXES, None), P(AXES, None)),
        out_specs=P(AXES, None),
        check_vma=False,
    )
```

```python
import functools

import jax
import jax.numpy as jnp
from jax import lax
from jax.experimental import pallas as pl
from jax.experimental.pallas import tpu as pltpu
from jax.sharding import Mesh
from jax.sharding import PartitionSpec as P

AXES = ("xl", "z", "y", "core", "grp")
SIZES = (2, 8, 4, 2, 2)
NODES = 64
MESH = pl.DeviceIdType.MESH
HIGHEST = lax.Precision.HIGHEST
PTS = 128
D = 4096
KNN = 16
QUARTER = 1024
WIDTHS = (256, 256, 256, 256)
CHUNKS = len(WIDTHS)
AHEAD = 3
STARTS = tuple(sum(WIDTHS[:j]) for j in range(CHUNKS))
FAR = 1e30
DEAD = 1e35
SUM_PHASES = ((3,), (0, 4, 2), (1,))


def sort_pairs(n):
    pairs = []
    p = 1
    while p < n:
        k = p
        while k >= 1:
            for j in range(k % p, n - k, 2 * k):
                for i in range(min(k, n - j - k)):
                    if (i + j) // (2 * p) == (i + j + k) // (2 * p):
                        pairs.append((i + j, i + j + k))
            k //= 2
        p *= 2
    return pairs


SORT16 = sort_pairs(KNN)


def sort_lists(values):
    values = list(values)
    for i, j in SORT16:
        low, high = jnp.minimum(values[i], values[j]), jnp.maximum(values[i], values[j])
        values[i], values[j] = low, high
    return values


def merge_lists(a, b):
    m = [jnp.minimum(a[i], b[KNN - 1 - i]) for i in range(KNN)]
    step = KNN // 2
    while step:
        for i in range(KNN):
            if not i & step:
                low, high = jnp.minimum(m[i], m[i + step]), jnp.maximum(m[i], m[i + step])
                m[i], m[i + step] = low, high
        step //= 2
    return m


def dot_nt(a, b):
    return lax.dot_general(
        a, b, (((1,), (1,)), ((), ())), precision=HIGHEST, preferred_element_type=jnp.float32
    )


def device_of(node, core, grp):
    return (node // 32, (node // 4) % 8, node % 4, core, grp)


def kernel(
    pts, cidx, ccnt, nbr, old, out,
    both, xr, fb, gx, gf, gb, gx_r, gf_r, gb_r, hx, hf, hb, rx, rv, rbv, ru,
    info, bias, tiles, nb_v, old_v, ci_v, nb_t, sum_src, sum_in,
    loc_sem, cc_v, sib_s, sib_r, x_s, x_r, yo_s, yr_s, f_r, info_s, info_r, red_s, red_r,
    via, via_s, via_r, t_s, rx_sem, rv_sem, rbv_sem, ru_sem, sum_s, sum_r,
):
    d = tuple(lax.axis_index(a) for a in AXES)
    c, g = d[3], d[4]
    q = d[0] * 32 + d[1] * 4 + d[2]
    up, down = (q + 1) % NODES, (q + NODES - 1) % NODES
    ahead = (q + NODES + 2 * c - 1) % NODES
    behind = (q + NODES + 1 - 2 * c) % NODES
    sibling = device_of(q, 1 - c, g)
    turned = d[0]

    def turn(bit, by):
        return bit + by - 2 * bit * by

    def quarter_at(core, grp):
        return 2 * turn(grp, core * turned) + core

    def same_quarter(node, core, grp):
        return device_of(node, core, turn(grp, core * turn(turned, node // 32)))

    mine_at = quarter_at(c, g)

    def remote(src, dst, send, recv, to):
        return pltpu.make_async_remote_copy(
            src_ref=src, dst_ref=dst, send_sem=send, recv_sem=recv, device_id=to, device_id_type=MESH
        )

    barrier = pltpu.get_barrier_semaphore()
    peers = [device_of(n, k, h) for n in (up, down) for k in (0, 1) for h in (0, 1)]
    peers.append(device_of(q, 1 - c, 1 - g))
    sum_peers = []
    for axes in SUM_PHASES:
        count = 1
        for a in axes:
            count *= SIZES[a]
        row = []
        for offset in range(1, count):
            at, rest = list(d), offset
            for a in axes:
                at[a] = (d[a] + rest % SIZES[a]) % SIZES[a]
                rest //= SIZES[a]
            row.append(tuple(at))
        sum_peers.append(row)
        peers += row
    ring = q % 32
    steps = ((c == 1) & (ring == 31)) | ((c == 0) & (ring == 0))
    passes = (ring == 0) | (ring == 31)
    onward = 1 - ring // 31
    middle = q + 31 - 62 * c
    source = device_of(q - 31 + 62 * onward, onward, g)
    after_node = (1 - d[0]) * 32 + 31 * (1 - onward)
    onward_to = same_quarter(after_node, c, g)

    def greet(peer):
        pl.semaphore_signal(barrier, inc=1, device_id=peer, device_id_type=MESH)

    for peer in peers:
        greet(peer)

    @pl.when(steps)
    def _():
        for k in (0, 1):
            greet(device_of(middle, k, g))

    @pl.when(passes)
    def _():
        greet(source)
        greet(onward_to)

    greeted = len(peers) + jnp.where(steps, 2, 0) + jnp.where(passes, 2, 0)
    loads = [
        pltpu.make_async_copy(pts, both.at[c], loc_sem.at[0]),
        pltpu.make_async_copy(cidx, ci_v, loc_sem.at[1]),
        pltpu.make_async_copy(nbr, nb_v, loc_sem.at[2]),
        pltpu.make_async_copy(old, old_v, loc_sem.at[3]),
        pltpu.make_async_copy(ccnt, cc_v, loc_sem.at[4]),
    ]
    for load in loads:
        load.start()
    pl.semaphore_wait(barrier, greeted)

    def cols(quarter, j):
        return pl.ds(pl.multiple_of(quarter * QUARTER + STARTS[j], 128), WIDTHS[j])

    def part(j):
        return pl.ds(STARTS[j], WIDTHS[j])

    def x_copy(k, j):
        return remote(
            pts.at[:, cols(quarter_at(k, 1 - g), j)], xr.at[c, :, part(j)], x_s.at[k, j], x_r.at[c, j],
            device_of(q, k, 1 - g),
        )

    def yo_copy(k, j):
        return remote(
            pts.at[:, cols(quarter_at(k, g), j)], fb.at[c, g, :, part(j)], yo_s.at[k, j], f_r.at[c, g, j],
            same_quarter(ahead, k, g),
        )

    def to_middle(k, j):
        return remote(
            pts.at[:, cols(quarter_at(k, g), j)], via.at[:, part(j)], yo_s.at[k, j], via_r.at[j],
            device_of(middle, k, g),
        )

    def pass_on(j):
        return remote(
            via.at[:, part(j)], fb.at[onward, g, :, part(j)], via_s.at[j], f_r.at[onward, g, j], onward_to
        )

    def sib_copy(i):
        quarter = pl.ds(pl.multiple_of(((quarter_at(1 - c, g) + i) % 4) * QUARTER, 128), QUARTER)
        return remote(pts.at[:, quarter], both.at[c, :, quarter], sib_s.at[i], sib_r.at[i], sibling)

    def relay(way, j):
        to = same_quarter(up if way else down, c, g)
        return remote(
            xr.at[way, :, part(j)], fb.at[way, 1 - g, :, part(j)], yr_s.at[way, j], f_r.at[way, 1 - g, j], to
        )

    def yo_start(k, j):
        @pl.when(steps)
        def _():
            to_middle(k, j).start()

        @pl.when(jnp.logical_not(steps))
        def _():
            yo_copy(k, j).start()

    for j in range(CHUNKS):
        for k in (0, 1):
            if j < AHEAD:
                x_copy(k, j).start()
                yo_start(k, j)
    for i in range(4):
        sib_copy(i).start()

    loads[1].wait()
    loads[4].wait()
    slot = lax.broadcasted_iota(jnp.int32, (PTS, PTS), 1)
    row = lax.broadcasted_iota(jnp.int32, (PTS, PTS), 0)
    hit = (jnp.broadcast_to(ci_v[...], (PTS, PTS)) == row) & (slot < cc_v[0])
    live = jnp.max(jnp.where(hit, 1.0, 0.0).T, axis=0, keepdims=True)
    loads[0].wait()
    square = jnp.zeros((PTS, PTS), jnp.float32)
    for i in range(D // PTS):
        x = both[c, :, i * PTS : (i + 1) * PTS]
        square = square + x * x
    norm = jnp.sum(square.T, axis=0, keepdims=True)
    info[0] = jnp.broadcast_to(jnp.where(live > 0.5, norm, DEAD), (8, PTS))
    info_to = [(sibling, 1)]
    info_to += [(device_of(q, k, 1 - g), 2 + c) for k in (0, 1)]
    info_to += [(device_of(ahead, k, h), 6 - 2 * c + g) for k in (0, 1) for h in (0, 1)]
    info_to += [(device_of(behind, c, h), 8 + g) for h in (0, 1)]
    info_sends = [
        remote(info.at[0], info.at[s], info_s.at[i], info_r.at[s], to) for i, (to, s) in enumerate(info_to)
    ]
    for send in info_sends:
        send.start()
    loads[2].wait()
    loads[3].wait()
    nb_t[...] = nb_v[...]
    old_t = old_v[...]

    def block_of(s):
        odd = s % 2
        far_pair = jnp.where(s < 8, 4 * up + odd, 4 * ahead + 2 * c + odd)
        far_pair = jnp.where(s < 6, 4 * down + 2 + odd, far_pair)
        near = jnp.where(s == 0, 4 * q + 2 * c + g, 4 * q + 2 * (1 - c) + g)
        near = jnp.where(s < 2, near, 4 * q + 2 * odd + 1 - g)
        return jnp.where(s < 4, near, far_pair)

    def set_bias(s):
        first = block_of(s) * PTS
        ids = first + lax.broadcasted_iota(jnp.int32, (PTS, PTS), 0)
        own_ids = (4 * q + 2 * c + g) * PTS + lax.broadcasted_iota(jnp.int32, (PTS, PTS), 1)
        masked = ids == own_ids
        for k in range(KNN):
            masked = masked | (ids == nb_t[k : k + 1, :])
        key = jnp.broadcast_to(info[s, 0:1, :], (PTS, PTS)).T
        bias[s] = jnp.where(masked, DEAD, key + norm)

    set_bias(0)
    for ref in (gx, gf, gb):
        ref[...] = jnp.zeros_like(ref)
    tiles[0] = jnp.zeros((PTS, PTS), jnp.float32)
    tiles[1] = jnp.zeros((PTS, PTS), jnp.float32)

    def near_blocks(core, j):
        return jnp.concatenate([both[core, :, cols(mine_at, j)], xr[core, :, part(j)]], axis=0)

    def far_products(j):
        for way in (0, 1):
            for h in (0, 1):
                remote(
                    xr.at[way, :, part(j)], fb.at[way, h, :, part(j)], yr_s.at[way, j], f_r.at[way, h, j], sibling
                ).wait_recv()
        f = fb[1, :, :, part(j)].reshape(2 * PTS, WIDTHS[j])
        gf[1 - c] += dot_nt(f, near_blocks(1 - c, j))
        if j == CHUNKS - 1:
            gf_copy.start()
        b = fb[0, :, :, part(j)].reshape(2 * PTS, WIDTHS[j])
        gb[...] += dot_nt(b, near_blocks(0, j))
        if j == CHUNKS - 1:
            pl.when(c == 1)(gb_copy.start)
        gf[c] += dot_nt(f, near_blocks(c, j))

    def far_quarter(j):
        sib_copy(j).wait_recv()
        quarter = pl.ds(pl.multiple_of(((mine_at + j) % 4) * QUARTER, 128), QUARTER)
        mine = both[c, :, quarter]
        tiles[0] += dot_nt(mine, mine)
        tiles[1] += dot_nt(both[1 - c, :, quarter], mine)

    gx_copy = remote(gx, gx_r, red_s.at[0], red_r.at[0], sibling)
    gf_copy = remote(gf.at[1 - c], gf_r, red_s.at[1], red_r.at[1], sibling)
    gb_copy = remote(gb, gb_r, red_s.at[2], red_r.at[2], sibling)

    for j in range(CHUNKS):

        @pl.when(passes)
        def _(j=j):
            to_middle(0, j).wait_recv()
            pass_on(j).start()

        for way in (0, 1):
            remote(
                pts.at[:, cols(0, j)], xr.at[way, :, part(j)], x_s.at[0, j], x_r.at[way, j], sibling
            ).wait_recv()
            relay(way, j).start()
        if j + AHEAD < CHUNKS:
            for k in (0, 1):
                x_copy(k, j + AHEAD).start()
                yo_start(k, j + AHEAD)
        for i in range(4):
            if max(i - 1, 0) == j:
                far_quarter(i)
        xs = jnp.concatenate([xr[0, :, part(j)], xr[1, :, part(j)]], axis=0)
        own = jnp.concatenate([both[0, :, cols(mine_at, j)], both[1, :, cols(mine_at, j)]], axis=0)
        gx[...] += dot_nt(xs, own)
        if j == CHUNKS - 2:
            def each(s, carry):
                remote(info.at[0], info.at[s], info_s.at[0], info_r.at[s], sibling).wait_recv()
                set_bias(s)
                return carry

            lax.fori_loop(1, 10, each, 0)
        if j == CHUNKS - 1:
            gx_copy.start()
        if j > 0:
            far_products(j - 1)

    gx_copy.wait_recv()
    total = gx[...] + gx_r[...]
    for k in (0, 1):
        hx[k] = total[k * PTS : (k + 1) * PTS]
    other = device_of(q, c, 1 - g)
    rx_copy = remote(hx.at[c], rx, t_s.at[0], rx_sem, other)
    rx_copy.start()

    far_products(CHUNKS - 1)
    gf_copy.wait_recv()
    total = gf[c] + gf_r[...]
    for rel in (0, 1):
        hf[rel] = total[:, rel * PTS : (rel + 1) * PTS]
    rv_copy = remote(hf.at[1], rv, t_s.at[1], rv_sem, other)
    rv_copy.start()

    def ru_copy(src, half_slot, rel, h, sem, to):
        name = g if rel == 0 else 1 - g
        return remote(
            src.at[rel, pl.ds(pl.multiple_of(h * PTS, PTS), PTS)], ru.at[g, half_slot, name], sem, ru_sem.at[g, half_slot, name], to
        )

    fu_copies = [
        ru_copy(hf, c, rel, h, t_s.at[2 + rel + 2 * i], device_of(down, 1, h))
        for i, h in enumerate((1 - g, g))
        for rel in (0, 1)
    ]
    for copy in fu_copies:
        copy.start()
    rbv_copy = remote(hb.at[1], rbv, t_s.at[6], rbv_sem, device_of(q, 0, 1 - g))
    bu_copies = [
        ru_copy(hb, 1, rel, h, t_s.at[7 + rel + 2 * i], device_of(up, 0, h))
        for i, h in enumerate((1 - g, g))
        for rel in (0, 1)
    ]

    @pl.when(c == 0)
    def _():
        gb_copy.wait_recv()
        for rel in (0, 1):
            half = pl.ds(rel * PTS, PTS)
            hb[rel] = gb[:, half] + gb_r[:, half]
        rbv_copy.start()
        for copy in bu_copies:
            copy.start()

    def taken(best, s, inner):
        value = bias[s]
        dist = jnp.where(value >= 1e34, FAR, (value - 2.0 * inner) / D)
        return merge_lists(best, sort_lists([dist[8 * i : 8 * i + 8] for i in range(KNN)]))

    low, high = jnp.minimum(old_t[:8], old_t[8:]), jnp.maximum(old_t[:8], old_t[8:])
    best = [low, high] + [jnp.full((8, PTS), FAR, jnp.float32)] * (KNN - 2)
    best = taken(best, 0, tiles[0])
    best = taken(best, 1, tiles[1])
    rx_copy.wait_recv()
    lanes = pl.ds(pl.multiple_of(c * PTS, PTS), PTS)
    for k in (0, 1):
        best = taken(best, 2 + k, hx[k, :, lanes] + rx[:, k * PTS : (k + 1) * PTS].T)
    rv_copy.wait_recv()
    for h in (0, 1):
        best = taken(best, 4 + h, hf[0, h * PTS : (h + 1) * PTS] + rv[h * PTS : (h + 1) * PTS])

    def wait_ru(half_slot):
        for half in (0, 1):
            for name in (0, 1):
                remote(
                    hf.at[0, pl.ds(0, PTS)], ru.at[half, half_slot, name], t_s.at[2], ru_sem.at[half, half_slot, name],
                    sibling,
                ).wait_recv()

    @pl.when(c == 0)
    def _():
        rbv_copy.wait_recv()
        for h in (0, 1):
            tiles[2 + h] = hb[0, h * PTS : (h + 1) * PTS] + rbv[h * PTS : (h + 1) * PTS]

    @pl.when(c == 1)
    def _():
        wait_ru(0)
        for h in (0, 1):
            tiles[2 + h] = (ru[0, 0, h] + ru[1, 0, h]).T

    for h in (0, 1):
        best = taken(best, 6 + h, tiles[2 + h])
    wait_ru(1)
    for h in (0, 1):
        best = taken(best, 8 + h, (ru[0, 1, h] + ru[1, 1, h]).T)
    for shift in (4, 2, 1):
        best = merge_lists(best, [pltpu.roll(v, shift, 0) for v in best])

    running = best[KNN - 1][0:1, :]
    sum_copies = []
    first = 0
    for phase, row_peers in enumerate(sum_peers):
        sum_src[phase] = running
        copies = [
            remote(sum_src.at[phase], sum_in.at[first + i], sum_s.at[first + i], sum_r.at[first + i], peer)
            for i, peer in enumerate(row_peers)
        ]
        for copy in copies:
            copy.start()
        for copy in copies:
            copy.wait_recv()
        for i in range(len(copies)):
            running = running + sum_in[first + i]
        sum_copies += copies
        first += len(copies)
    mean = jnp.sum(running, axis=1, keepdims=True) / (PTS * NODES * 4)
    for k in range(KNN):
        out[k : k + 1, :] = best[k][0:1, :] / mean

    for j in range(CHUNKS):
        for k in (0, 1):
            x_copy(k, j).wait_send()
            yo_copy(k, j).wait_send()
            relay(k, j).wait_send()

        @pl.when(passes)
        def _(j=j):
            pass_on(j).wait_send()

    for i in range(4):
        sib_copy(i).wait_send()
    for send in info_sends:
        send.wait_send()
    for copy in [gx_copy, gf_copy, rx_copy, rv_copy, *fu_copies, *sum_copies]:
        copy.wait_send()

    @pl.when(c == 1)
    def _():
        gb_copy.wait_send()

    @pl.when(c == 0)
    def _():
        rbv_copy.wait_send()
        for copy in bu_copies:
            copy.wait_send()


def body(points, cand_index, cand_count, neighbor_ids, old_dist):
    f32, dma = jnp.float32, pltpu.SemaphoreType.DMA
    n_sum = 1 + 15 + 7
    vmem = pltpu.VMEM
    any_spec = pl.BlockSpec(memory_space=pltpu.HBM)
    scratch = [
        vmem((2, PTS, D), f32),
        vmem((2, PTS, QUARTER), f32),
        vmem((2, 2, PTS, QUARTER), f32),
        vmem((256, 256), f32),
        vmem((2, 256, 256), f32),
        vmem((256, 256), f32),
        vmem((256, 256), f32),
        vmem((256, 256), f32),
        vmem((256, 256), f32),
        vmem((2, 128, 256), f32),
        vmem((2, 256, 128), f32),
        vmem((2, 256, 128), f32),
        vmem((128, 256), f32),
        vmem((256, 128), f32),
        vmem((256, 128), f32),
        vmem((2, 2, 2, 128, 128), f32),
        vmem((10, 8, 128), f32),
        vmem((10, 128, 128), f32),
        vmem((4, 128, 128), f32),
        vmem((16, 128), jnp.int32),
        vmem((16, 128), f32),
        vmem((1, 128), jnp.int32),
        vmem((16, 128), jnp.int32),
        vmem((3, 1, 128), f32),
        vmem((n_sum, 1, 128), f32),
        dma((5,)),
        pltpu.SMEM((1,), jnp.int32),
        dma((CHUNKS,)),
        dma((CHUNKS,)),
        dma((2, CHUNKS)),
        dma((2, CHUNKS)),
        dma((2, CHUNKS)),
        dma((2, CHUNKS)),
        dma((2, 2, CHUNKS)),
        dma((9,)),
        dma((10,)),
        dma((3,)),
        dma((3,)),
        vmem((PTS, QUARTER), f32),
        dma((CHUNKS,)),
        dma((CHUNKS,)),
        dma((11,)),
        dma,
        dma,
        dma,
        dma((2, 2, 2)),
        dma((n_sum,)),
        dma((n_sum,)),
    ]
    best = pl.pallas_call(
        kernel,
        out_shape=jax.ShapeDtypeStruct((KNN, PTS), f32),
        in_specs=[any_spec] * 5,
        out_specs=pl.BlockSpec(memory_space=pltpu.VMEM),
        scratch_shapes=scratch,
        compiler_params=pltpu.CompilerParams(
            collective_id=0, has_side_effects=True, vmem_limit_bytes=40 << 20
        ),
    )(points, cand_index, cand_count, neighbor_ids.T, old_dist.T)
    return best.T


def solution(mesh):
    finer = Mesh(mesh.devices.reshape(*SIZES), AXES)
    return jax.shard_map(
        body,
        mesh=finer,
        in_specs=(P(AXES, None), P(AXES, None), P(AXES), P(AXES, None), P(AXES, None)),
        out_specs=P(AXES, None),
        check_vma=False,
    )
```
